128 devices in a mesh: dp: 8 (over z, x_hi), expert: 16 (over y, x_lo, core).
Axes of the slice: x: 4 (x_hi: 2, x_lo: 2; x = x_hi * 2 + x_lo), y: 4, z: 4, core: 2. Of those that a mesh axis runs over, the one named last changes fastest.
Arguments:
- activations: bfloat16 [16, 8192, 2048], P('expert', 'dp'), may hold values from -6 to 6
- grad_hidden: bfloat16 [16, 8192, 1536], P('expert', 'dp'), may hold values from -6 to 6
- counts: int32 [16, 8], P('expert', 'dp'), may hold values from 1 to 1024, as said below
- master: float32 [16, 2048, 1536], P('expert', 'dp'), may hold values from -0.125 to 0.125
- moment1: float32 [16, 2048, 1536], P('expert', 'dp'), may hold values from -3 to 3
- moment2: float32 [16, 2048, 1536], P('expert', 'dp'), may hold values from 0.01 to 1
- old_slot: int32 [16], replicated, may hold values from 0 to 15, each once
- new_slot: int32 [16], replicated, may hold values from 0 to 15, each once
Outputs:
- master_out: float32 [16, 2048, 1536], P('expert', 'dp')
- moment1_out: float32 [16, 2048, 1536], P('expert', 'dp')
- moment2_out: float32 [16, 2048, 1536], P('expert', 'dp')
- new_weight: bfloat16 [16, 2048, 1536], P('expert')
The draws below stay inside these ranges and needn't reach their ends.
Inputs may be any that keep to these rules, and one draw needn't show every extreme that they name: `counts`: each entry is at most 1024, and some entry equals 1024.
All inputs are finite; a program needn't handle non-finite values.
Results may differ from the reference program's by a relative error of at most 0.0055.
Values may be sent and summed in bfloat16 or wider, within the bound.
A program may use at most 128 MiB of HBM per device.

```python
import math
import jax
import jax.numpy as jnp
from jax import lax

D = 2048
FF = 768
TOK_DEV = 1024
EXPERTS = 16
ROWS = 8192
N_DP = 8


def draw_counts(key, part):
    count_key, spot_key = jax.random.split(jax.random.fold_in(key, 17))
    base_counts = jax.random.randint(count_key, (EXPERTS * N_DP,), 1, TOK_DEV + 1)
    full_spot = jax.random.randint(spot_key, (), 0, EXPERTS * N_DP)
    flat_counts = jnp.where(jnp.arange(EXPERTS * N_DP) == full_spot, TOK_DEV, base_counts)
    return flat_counts.reshape(EXPERTS, N_DP).astype(jnp.int32)


def with_spikes(entries, own_key, source, target, shards_of, factor):
    owner, partner = [(jnp.arange(entries.shape[axis_at]) // (entries.shape[axis_at] // shards_of)).reshape([-1 if axis == axis_at else 1 for axis in range(entries.ndim)]) for axis_at in (source, target)]
    chosen = jax.random.permutation(own_key, shards_of)[partner]
    strong = (owner == chosen) | (owner == (partner + shards_of // 2) % shards_of)
    return jnp.where(strong, factor * entries, entries)


def shard_levels(rng, shape, pieces, low, top_value):
    gain = 1.0
    for position, parts in pieces:
        draws = jax.random.uniform(jax.random.fold_in(jax.random.fold_in(rng, 6), position), (parts,), jnp.float32, low / len(pieces), top_value / len(pieces))
        gain = gain * jnp.repeat(jnp.exp(draws), shape[position] // parts).reshape((-1,) + (1,) * (len(shape) - 1 - position))
    return gain


def bell_draw(stream_key, shape, spread, bound, cuts=(), held_as=jnp.bfloat16):
    gain = shard_levels(stream_key, shape, cuts, -0.22, 0.18) if cuts else 1.0
    values = jax.random.normal(stream_key, shape, jnp.float32) * spread * gain
    return jnp.minimum(jnp.maximum(values, -bound), bound).astype(held_as)


def gaussian_with(rng, dims, spread, bound, cuts, heavy, held_as=jnp.bfloat16):
    result = spread * jax.random.normal(rng, dims, jnp.float32)
    if cuts:
        result = result * shard_levels(rng, dims, cuts, -0.22, 0.18)
    return jnp.clip(with_spikes(result, jax.random.fold_in(rng, 3), *heavy), -bound, bound).astype(held_as)


def setup_inputs(seed: int = 0) -> dict:
    splits = jax.random.split(jax.random.key(seed), 9)
    return {
        "activations": gaussian_with(splits[0], (EXPERTS, ROWS, D), 1.0, 6.0, ((0, 16), (1, 8)), (1, 2, 8, 2.0)),
        "grad_hidden": bell_draw(splits[1], (EXPERTS, ROWS, 2 * FF), 1.0, 6.0, ((0, 16), (1, 8))),
        "counts": draw_counts(jax.random.fold_in(splits[8], 71), 0),
        "master": bell_draw(splits[3], (EXPERTS, D, 2 * FF), D ** -0.5, 0.125, ((0, 16), (1, 8)), jnp.float32),
        "moment1": bell_draw(splits[4], (EXPERTS, D, 2 * FF), 0.3, 3.0, ((0, 16), (1, 8)), jnp.float32),
        "moment2": jnp.clip(jnp.exp(math.log(1.0) - 4.6051702 * jax.random.uniform(splits[5], (EXPERTS, D, 2 * FF), jnp.float32) ** shard_levels(splits[5], (EXPERTS, D, 2 * FF), ((0, 16), (1, 8)), -0.2, 0.2)), 0.01, 1.0),
        "old_slot": jax.random.permutation(splits[6], EXPERTS).astype(jnp.int32),
        "new_slot": jax.random.permutation(splits[7], EXPERTS).astype(jnp.int32),
    }


beta_one = 0.9
beta_two = 0.95
learn_rate = 0.01
decay_rate = 0.1
adam_eps = 1e-08
step_number = 20

def source_slots(old_slot, new_slot):
    slots = old_slot.shape[0]
    wanted = jnp.arange(slots, dtype=jnp.int32)
    picked = jnp.where(new_slot[None, :] == wanted[:, None], old_slot[None, :], 0)
    return lax.optimization_barrier(jnp.sum(picked, axis=1)).astype(jnp.int32)

def adamw(grads, master, moment1, moment2):
    first = beta_one * moment1 + (1.0 - beta_one) * grads
    second = beta_two * moment2 + (1.0 - beta_two) * grads * grads
    first_hat = first / (1.0 - beta_one ** step_number)
    second_hat = second / (1.0 - beta_two ** step_number)
    updated = master - learn_rate * (first_hat / (jnp.sqrt(second_hat) + adam_eps) + decay_rate * master)
    return (updated, first, second)

def reference(activations, grad_hidden, counts, master, moment1, moment2, old_slot, new_slot):
    rows_all = activations.shape[1]
    row_index = jnp.arange(rows_all, dtype=jnp.int32)

    def slot_grad(slot_data):
        inputs, cot_in, slot_counts = slot_data
        limits = jnp.take(slot_counts, (row_index // TOK_DEV).astype(jnp.int32))
        keep = row_index % TOK_DEV < limits
        cotangent = jnp.where(keep[:, None], cot_in, jnp.zeros((), jnp.bfloat16))
        return lax.dot_general(inputs, cotangent, (((0,), (0,)), ((), ())), preferred_element_type=jnp.float32)
    grads = lax.map(slot_grad, (activations, grad_hidden, counts)) / math.sqrt(rows_all)
    updated, first, second = adamw(grads, master, moment1, moment2)
    new_weight = jnp.take(updated.astype(jnp.bfloat16), source_slots(old_slot, new_slot), axis=0)
    return (updated, first, second, new_weight)
```

```python
import functools
import math

import jax
import jax.numpy as jnp
from jax import lax
from jax.experimental import pallas as pl
from jax.experimental.pallas import tpu as pltpu
from jax.sharding import Mesh
from jax.sharding import PartitionSpec as P

MESH = pl.DeviceIdType.MESH
AXES = ("z", "xh", "y", "xl", "c")
EXPERT = ("y", "xl", "c")
DP = ("z", "xh")

beta_one = 0.9
beta_two = 0.95
learn_rate = 0.01
decay_rate = 0.1
adam_eps = 1e-08
step_number = 20


def source_slots(old_slot, new_slot):
    slots = old_slot.shape[0]
    wanted = jnp.arange(slots, dtype=jnp.int32)
    picked = jnp.where(new_slot[None, :] == wanted[:, None], old_slot[None, :], 0)
    return jnp.sum(picked, axis=1)


def adamw(grads, master, moment1, moment2):
    first = beta_one * moment1 + (1.0 - beta_one) * grads
    second = beta_two * moment2 + (1.0 - beta_two) * grads * grads
    first_hat = first / (1.0 - beta_one**step_number)
    second_hat = second / (1.0 - beta_two**step_number)
    updated = master - learn_rate * (
        first_hat / (jnp.sqrt(second_hat) + adam_eps) + decay_rate * master
    )
    return (updated, first, second)


class Counter:
    def __init__(self):
        self.used = 0

    def take(self):
        self.used += 1
        return self.used - 1


def copies_in_all(slots):
    chunk_a = 6 + 1 + 2 * (slots - 1) + 1 + 6
    chunk_b = 8 + 6 + 2 * (slots - 1) + 6 + 7
    return 2 * chunk_a + chunk_b


def kernel(
    sizes,
    source_ref,
    count_ref,
    act_hbm,
    grad_hbm,
    master_hbm,
    first_hbm,
    second_hbm,
    master_out,
    first_out,
    second_out,
    weight_out,
    act_raw,
    act_t,
    grad_raw,
    cot,
    states,
    outs,
    ring_send_a,
    ring_recv_a,
    cross_send_a,
    cross_recv_a,
    own_a,
    cross_send_b,
    cross_recv_b,
    ring_send_b,
    ring_recv_b,
    own_b,
    updated_w,
    spread_0,
    spread_1,
    spread_2,
    chosen,
    weight,
    load_sem,
    store_sem,
    send_sem,
    recv_sem,
):
    ny, nl, nc, rows, half_w, tokens, scale = sizes
    spread = (spread_0, spread_1, spread_2)
    slots = ny * nl * nc
    piece = rows // slots
    block = 2 * rows
    wide = 2 * half_w
    z, xh, y, xl, c = (lax.axis_index(a) for a in AXES)
    me = (y * nl + xl) * nc + c
    dp_row = (z * 2 + xh) * rows
    step = min(128, rows)

    def device(zz=None, xx=None, slot=None):
        yy, ll, cc = slot if slot is not None else (y, xl, c)
        return (z if zz is None else zz, xh if xx is None else xx, yy, ll, cc)

    z_next = lax.rem(z + 1, 4)
    z_prev = lax.rem(z + 3, 4)
    toward = (device(zz=z_next), device(zz=z_prev))
    across = device(xx=1 - xh)
    others = []
    for jy in range(ny):
        for jl in range(nl):
            for jc in range(nc):
                if jy or jl or jc:
                    slot = (lax.rem(y + jy, ny), lax.rem(xl + jl, nl), lax.rem(c + jc, nc))
                    others.append((device(slot=slot), (slot[0] * nl + slot[1]) * nc + slot[2]))

    loads = []

    def load(src, dst):
        cp = pltpu.make_async_copy(src, dst, load_sem.at[len(loads)])
        cp.start()
        loads.append(cp)
        return cp

    def load_act(rel):
        base = lax.rem(z + rel, 4) * block
        got = []
        for part, at in ((0, xh), (1, 1 - xh)):
            cols = pl.ds(pl.multiple_of(base + at * rows, rows), rows)
            got.append(load(act_hbm.at[:, cols], act_raw.at[rel, :, pl.ds(part * rows, rows)]))
        return got

    def load_grad(chunk):
        cols = pl.ds(chunk * wide, wide)
        return load(grad_hbm.at[:, cols], grad_raw.at[:, cols])

    got_grad = {0: load_grad(0)}
    got_act = {3: load_act(3), 1: load_act(1)}
    got_grad[2] = load_grad(2)
    got_grad[1] = load_grad(1)
    got_act[2] = load_act(2)
    got_act[0] = load_act(0)
    got_states = [
        load(ref, states.at[n]) for n, ref in enumerate((master_hbm, first_hbm, second_hbm))
    ]

    barrier = pltpu.get_barrier_semaphore()
    partners = [toward[0], toward[1], across] + [dev for dev, _ in others]
    for dev in partners:
        pl.semaphore_signal(barrier, inc=1, device_id=dev, device_id_type=MESH)

    live = count_ref[0]

    def mask_grad(chunk):
        got_grad[chunk].wait()
        keep = lax.broadcasted_iota(jnp.int32, (tokens, 128), 0) < live
        for j in range(wide // 128):
            cols = pl.ds(chunk * wide + j * 128, 128)
            part = grad_raw[:, cols]
            cot[:, cols] = jnp.where(keep, part, jnp.zeros_like(part))

    def turn(rel):
        for cp in got_act[rel]:
            cp.wait()

        def one(i, carry):
            at = pl.ds(pl.multiple_of(i * 128, 128), 128)
            act_t[rel, at, :] = act_raw[rel, :, at].T
            return carry

        lax.fori_loop(0, block // 128, one, 0)

    def product(rel, row0, count, col0, width, write, terms=()):
        def one(i, carry):
            at = pl.multiple_of(i * step, step)
            total = jnp.dot(
                act_t[rel, pl.ds(row0 + at, step), :],
                cot[:, pl.ds(col0, width)],
                preferred_element_type=jnp.float32,
            )
            for term in terms:
                total = total + term(at).astype(jnp.float32)
            write(at, total)
            return carry

        lax.fori_loop(0, count // step, one, 0)

    counter = Counter()
    sends = []

    def send(src, dst, dev):
        n = counter.take()
        cp = pltpu.make_async_remote_copy(
            src_ref=src,
            dst_ref=dst,
            send_sem=send_sem.at[n],
            recv_sem=recv_sem.at[n],
            device_id=dev,
            device_id_type=MESH,
        )
        cp.start()
        sends.append(cp)
        return cp

    order = ((3, 2, 1, 0), (1, 2, 3, 0))
    ring = {}

    def ring_a(chunk, s, dirs=(0, 1)):
        for dr in dirs:
            col0 = chunk * wide + dr * half_w
            rel = order[dr][s]
            terms = ()
            if s:
                ring[chunk, dr, s - 1].wait_recv()
                terms = (lambda at, dr=dr: ring_recv_a[chunk, dr, s - 1, pl.ds(at, step), :],)
            if s < 3:

                def write(at, total, dr=dr):
                    ring_send_a[chunk, dr, s, pl.ds(at, step), :] = total.astype(jnp.bfloat16)

                product(rel, 0, block, col0, half_w, write, terms)
                ring[chunk, dr, s] = send(
                    ring_send_a.at[chunk, dr, s], ring_recv_a.at[chunk, dr, s], toward[dr]
                )
            else:

                def write_far(at, total, dr=dr):
                    cross_send_a[chunk, pl.ds(at, step), pl.ds(dr * half_w, half_w)] = total.astype(
                        jnp.bfloat16
                    )

                def write_own(at, total, dr=dr):
                    own_a[chunk, pl.ds(at, step), pl.ds(dr * half_w, half_w)] = total

                far = (
                    lambda at, dr=dr: ring_recv_a[chunk, dr, s - 1, pl.ds(at + rows, step), :],
                )
                product(rel, rows, rows, col0, half_w, write_far, far)
                product(rel, 0, rows, col0, half_w, write_own, terms)
        if s == 3:
            ring[chunk, "x"] = send(cross_send_a.at[chunk], cross_recv_a.at[chunk], across)

    def cross_b(dr, s):
        rel = order[dr][s]

        def write(at, total):
            cross_send_b[dr, s, pl.ds(at, step), :] = total.astype(jnp.bfloat16)

        product(rel, rows, rows, 2 * wide + dr * half_w, half_w, write)
        ring["b", "x", dr, s] = send(cross_send_b.at[dr, s], cross_recv_b.at[dr, s], across)

    def ring_b(s):
        for dr in (0, 1):
            ring["b", "x", dr, s].wait_recv()
            terms = [lambda at, dr=dr: cross_recv_b[dr, s, pl.ds(at, step), :]]
            if s:
                ring["b", dr, s - 1].wait_recv()
                terms.append(lambda at, dr=dr: ring_recv_b[dr, s - 1, pl.ds(at, step), :])
            if s < 3:

                def write(at, total, dr=dr):
                    ring_send_b[dr, s, pl.ds(at, step), :] = total.astype(jnp.bfloat16)
            else:

                def write(at, total, dr=dr):
                    own_b[pl.ds(at, step), pl.ds(dr * half_w, half_w)] = total

            product(order[dr][s], 0, rows, 2 * wide + dr * half_w, half_w, write, terms)
            if s < 3:
                ring["b", dr, s] = send(ring_send_b.at[dr, s], ring_recv_b.at[dr, s], toward[dr])

    stores = []

    def store(src, dst):
        cp = pltpu.make_async_copy(src, dst, store_sem.at[len(stores)])
        cp.start()
        stores.append(cp)

    spreads = {}

    def update(chunk):
        if chunk < 2:
            ring[chunk, "x"].wait_recv()
        cols = pl.ds(chunk * wide, wide)
        few = min(32, rows)

        def one(i, carry):
            at = pl.ds(pl.multiple_of(i * few, few), few)
            if chunk < 2:
                total = own_a[chunk, at, :] + cross_recv_a[chunk, at, :].astype(jnp.float32)
            else:
                total = own_b[at, :]
            new, first, second = adamw(
                total * scale, states[0, at, cols], states[1, at, cols], states[2, at, cols]
            )
            outs[0, at, cols] = new
            outs[1, at, cols] = first
            outs[2, at, cols] = second
            updated_w[chunk, at, :] = new.astype(jnp.bfloat16)
            return carry

        lax.fori_loop(0, rows // few, one, 0)
        spreads[chunk] = [
            send(
                updated_w.at[chunk, pl.ds(pl.multiple_of(slot * piece, piece), piece)],
                spread[chunk].at[me],
                dev,
            )
            for dev, slot in others
        ]
        spread[chunk][me] = updated_w[chunk, pl.ds(pl.multiple_of(me * piece, piece), piece), :]
        for n, ref in enumerate((master_out, first_out, second_out)):
            store(outs.at[n, :, cols], ref.at[:, cols])

    moves = {}

    def move(chunk):
        for cp in spreads[chunk]:
            cp.wait_recv()
        cols = pl.ds(chunk * wide, wide)
        for k in range(slots):
            chosen[chunk, k] = spread[chunk][source_ref[k]]
        here = pl.ds(pl.multiple_of(dp_row + me * piece, piece), piece)
        moves[chunk] = [
            send(chosen.at[chunk, slot], weight.at[here, cols], dev) for dev, slot in others
        ]
        weight[here, cols] = chosen[chunk, me]

    def land(chunk, row0, count, col0, width):
        at = (pl.ds(row0, count), pl.ds(col0, width))
        store(weight.at[at], weight_out.at[at])

    gather = {}

    def moved(chunk):
        for cp in moves[chunk]:
            cp.wait_recv()
        here = pl.ds(pl.multiple_of(dp_row, rows), rows)
        cols = pl.ds(chunk * wide, wide)
        if chunk < 2:
            gather[chunk, "x"] = send(weight.at[here, cols], weight.at[here, cols], across)
        else:
            for dr in (0, 1):
                part = pl.ds(chunk * wide + dr * half_w, half_w)
                gather["b", dr, 0] = send(weight.at[here, part], weight.at[here, part], toward[dr])
            gather["b", "x", 0] = send(weight.at[here, cols], weight.at[here, cols], across)

    def gather_a(chunk, s):
        for dr in (0, 1):
            back = (4 - s) if dr == 0 else s
            row0 = pl.multiple_of(lax.rem(z + back, 4) * block, block)
            at = (pl.ds(row0, block), pl.ds(chunk * wide + dr * half_w, half_w))
            if s == 0:
                if dr == 0:
                    gather[chunk, "x"].wait_recv()
            else:
                gather[chunk, dr, s - 1].wait_recv()
            if s < 3:
                gather[chunk, dr, s] = send(weight.at[at], weight.at[at], toward[dr])
            store(weight.at[at], weight_out.at[at])

    def gather_b(s):
        for dr in (0, 1):
            back = (4 - s) if dr == 0 else s
            row0 = pl.multiple_of((lax.rem(z + back, 4) * 2 + xh) * rows, rows)
            at = (pl.ds(row0, rows), pl.ds(2 * wide + dr * half_w, half_w))
            gather["b", dr, s - 1].wait_recv()
            if s < 3:
                gather["b", dr, s] = send(weight.at[at], weight.at[at], toward[dr])
            gather["b", "x", dr, s] = send(weight.at[at], weight.at[at], across)

    def end_b():
        gather["b", "x", 0].wait_recv()
        for s in (1, 2, 3):
            for dr in (0, 1):
                gather["b", "x", dr, s].wait_recv()
        cols = pl.ds(2 * wide, wide)
        store(weight.at[:, cols], weight_out.at[:, cols])

    mask_grad(0)
    turn(3)
    pl.semaphore_wait(barrier, len(partners))
    ring_a(0, 0, (0,))
    turn(1)
    ring_a(0, 0, (1,))
    mask_grad(2)
    cross_b(0, 0)
    cross_b(1, 0)
    mask_grad(1)
    ring_a(1, 0)
    turn(2)
    cross_b(0, 1)
    cross_b(1, 1)
    cross_b(0, 2)
    cross_b(1, 2)
    turn(0)
    cross_b(0, 3)
    cross_b(1, 3)
    ring_b(0)
    ring_a(0, 1)
    ring_b(1)
    ring_a(0, 2)
    ring_b(2)
    ring_a(1, 1)
    ring_a(0, 3)
    for cp in got_states:
        cp.wait()
    ring_b(3)
    update(2)
    update(0)
    ring_a(1, 2)
    move(2)
    move(0)
    ring_a(1, 3)
    moved(2)
    moved(0)
    update(1)
    gather_b(1)
    gather_a(0, 0)
    move(1)
    gather_b(2)
    gather_a(0, 1)
    moved(1)
    gather_b(3)
    gather_a(1, 0)
    gather_a(0, 2)
    gather_a(1, 1)
    gather_a(0, 3)
    gather_a(1, 2)
    end_b()
    gather_a(1, 3)
    for cp in sends:
        cp.wait_send()
    for cp in stores:
        cp.wait()


def solution(mesh):
    finer = Mesh(mesh.devices.reshape(4, 2, 4, 2, 2), AXES)
    return build(finer)


def build(finer):
    ny, nl, nc = (finer.shape[a] for a in EXPERT)
    slots = ny * nl * nc

    def on_device(act, grad, counts, master, moment1, moment2, old_slot, new_slot):
        tokens, width = act.shape[1], act.shape[2]
        columns = grad.shape[2]
        rows = width // 8
        half_w = columns // 6
        wide = 2 * half_w
        block = 2 * rows
        piece = rows // slots
        bf, f32 = jnp.bfloat16, jnp.float32
        sizes = (ny, nl, nc, rows, half_w, tokens, 1.0 / math.sqrt(tokens * 8))
        any_spec = pl.BlockSpec(memory_space=pl.ANY)
        smem = pl.BlockSpec(memory_space=pltpu.SMEM)
        copies = copies_in_all(slots)
        state = jax.ShapeDtypeStruct((rows, columns), f32)
        new, first, second, moved = pl.pallas_call(
            functools.partial(kernel, sizes),
            out_shape=(state, state, state, jax.ShapeDtypeStruct((width, columns), bf)),
            in_specs=[smem, smem] + [any_spec] * 5,
            out_specs=(any_spec,) * 4,
            scratch_shapes=[
                pltpu.VMEM((4, tokens, block), bf),
                pltpu.VMEM((4, block, tokens), bf),
                pltpu.VMEM((tokens, columns), bf),
                pltpu.VMEM((tokens, columns), bf),
                pltpu.VMEM((3, rows, columns), f32),
                pltpu.VMEM((3, rows, columns), f32),
                pltpu.VMEM((2, 2, 3, block, half_w), bf),
                pltpu.VMEM((2, 2, 3, block, half_w), bf),
                pltpu.VMEM((2, rows, wide), bf),
                pltpu.VMEM((2, rows, wide), bf),
                pltpu.VMEM((2, rows, wide), f32),
                pltpu.VMEM((2, 4, rows, half_w), bf),
                pltpu.VMEM((2, 4, rows, half_w), bf),
                pltpu.VMEM((2, 3, rows, half_w), bf),
                pltpu.VMEM((2, 3, rows, half_w), bf),
                pltpu.VMEM((rows, wide), f32),
                pltpu.VMEM((3, rows, wide), bf),
                pltpu.VMEM((slots, piece, wide), bf),
                pltpu.VMEM((slots, piece, wide), bf),
                pltpu.VMEM((slots, piece, wide), bf),
                pltpu.VMEM((3, slots, piece, wide), bf),
                pltpu.VMEM((width, columns), bf),
                pltpu.SemaphoreType.DMA((14,)),
                pltpu.SemaphoreType.DMA((26,)),
                pltpu.SemaphoreType.DMA((copies,)),
                pltpu.SemaphoreType.DMA((copies,)),
            ],
            compiler_params=pltpu.CompilerParams(
                collective_id=0, has_side_effects=True, vmem_limit_bytes=60 << 20
            ),
            name="step",
        )(
            source_slots(old_slot, new_slot),
            counts[0],
            act[0],
            grad[0],
            master[0],
            moment1[0],
            moment2[0],
        )
        return (new[None], first[None], second[None], moved[None])

    in_specs = (
        P(EXPERT, DP, None),
        P(EXPERT, DP, None),
        P(EXPERT, DP),
        P(EXPERT, DP, None),
        P(EXPERT, DP, None),
        P(EXPERT, DP, None),
        P(),
        P(),
    )
    out_specs = (
        P(EXPERT, DP, None),
        P(EXPERT, DP, None),
        P(EXPERT, DP, None),
        P(EXPERT, None, None),
    )
    return jax.shard_map(on_device, mesh=finer, in_specs=in_specs, out_specs=out_specs, check_vma=False)
```

```python
import functools
import math

import jax
import jax.numpy as jnp
from jax import lax
from jax.experimental import pallas as pl
from jax.experimental.pallas import tpu as pltpu
from jax.sharding import Mesh
from jax.sharding import PartitionSpec as P

MESH = pl.DeviceIdType.MESH
AXES = ("z", "xh", "y", "xl", "c")
EXPERT = ("y", "xl", "c")
DP = ("z", "xh")

beta_one = 0.9
beta_two = 0.95
learn_rate = 0.01
decay_rate = 0.1
adam_eps = 1e-08
step_number = 20


def adamw(grads, master, moment1, moment2):
    first = beta_one * moment1 + (1.0 - beta_one) * grads
    second = beta_two * moment2 + (1.0 - beta_two) * grads * grads
    first_hat = first / (1.0 - beta_one**step_number)
    second_hat = second / (1.0 - beta_two**step_number)
    updated = master - learn_rate * (
        first_hat / (jnp.sqrt(second_hat) + adam_eps) + decay_rate * master
    )
    return (updated, first, second)


class Counter:
    def __init__(self):
        self.used = 0

    def take(self):
        self.used += 1
        return self.used - 1


def copies_in_all(slots):
    chunk_a = 6 + 1 + 2 * (slots - 1) + 1 + 6
    chunk_b = 8 + 6 + 2 * (slots - 1) + 6 + 7
    return 2 * chunk_a + chunk_b


def kernel(
    sizes,
    old_ref,
    new_ref,
    count_ref,
    act_hbm,
    grad_hbm,
    master_hbm,
    first_hbm,
    second_hbm,
    master_out,
    first_out,
    second_out,
    weight,
    act_raw,
    act_t,
    grad_raw,
    cot,
    states,
    ring_send_a,
    ring_recv_a,
    cross_send_a,
    cross_recv_a,
    own_a,
    cross_send_b,
    cross_recv_b,
    ring_send_b,
    ring_recv_b,
    own_b,
    updated_w,
    spread_0,
    spread_1,
    spread_2,
    chosen,
    source,
    load_sem,
    send_sem,
    recv_sem,
):
    ny, nl, nc, rows, half_w, tokens, scale = sizes
    spread = (spread_0, spread_1, spread_2)
    slots = ny * nl * nc
    piece = rows // slots
    block = 2 * rows
    wide = 2 * half_w
    z, xh, y, xl, c = (lax.axis_index(a) for a in AXES)
    me = (y * nl + xl) * nc + c
    dp_row = (z * 2 + xh) * rows
    step = min(256, rows)

    def device(zz=None, xx=None, slot=None):
        yy, ll, cc = slot if slot is not None else (y, xl, c)
        return (z if zz is None else zz, xh if xx is None else xx, yy, ll, cc)

    z_next = lax.rem(z + 1, 4)
    z_prev = lax.rem(z + 3, 4)
    toward = (device(zz=z_next), device(zz=z_prev))
    across = device(xx=1 - xh)
    others = []
    for jy in range(ny):
        for jl in range(nl):
            for jc in range(nc):
                if jy or jl or jc:
                    slot = (lax.rem(y + jy, ny), lax.rem(xl + jl, nl), lax.rem(c + jc, nc))
                    others.append((device(slot=slot), (slot[0] * nl + slot[1]) * nc + slot[2]))

    loads = []

    def load(src, dst):
        cp = pltpu.make_async_copy(src, dst, load_sem.at[len(loads)])
        cp.start()
        loads.append(cp)
        return cp

    def load_act(rel):
        base = lax.rem(z + rel, 4) * block
        got = []
        for part, at in ((0, xh), (1, 1 - xh)):
            cols = pl.ds(pl.multiple_of(base + at * rows, rows), rows)
            got.append(load(act_hbm.at[:, cols], act_raw.at[rel, :, pl.ds(part * rows, rows)]))
        return got

    def load_grad(chunk):
        cols = pl.ds(chunk * wide, wide)
        return load(grad_hbm.at[:, cols], grad_raw.at[:, cols])

    got_grad = {0: load_grad(0)}
    got_act = {3: load_act(3), 1: load_act(1)}
    got_grad[2] = load_grad(2)
    got_grad[1] = load_grad(1)
    got_act[2] = load_act(2)
    got_act[0] = load_act(0)
    got_states = [
        load(ref, states.at[n]) for n, ref in enumerate((master_hbm, first_hbm, second_hbm))
    ]

    barrier = pltpu.get_barrier_semaphore()
    partners = [toward[0], toward[1], across] + [dev for dev, _ in others]
    for dev in partners:
        pl.semaphore_signal(barrier, inc=1, device_id=dev, device_id_type=MESH)

    live = count_ref[0]

    def mask_grad(chunk):
        got_grad[chunk].wait()
        keep = lax.broadcasted_iota(jnp.int32, (tokens, 128), 0) < live
        for j in range(wide // 128):
            cols = pl.ds(chunk * wide + j * 128, 128)
            part = grad_raw[:, cols]
            cot[:, cols] = jnp.where(keep, part, jnp.zeros_like(part))

    def turn(rel):
        for cp in got_act[rel]:
            cp.wait()

        def one(i, carry):
            at = pl.ds(pl.multiple_of(i * 128, 128), 128)
            act_t[rel, at, :] = act_raw[rel, :, at].T
            return carry

        lax.fori_loop(0, block // 128, one, 0)

    def product(rel, row0, count, col0, width, write, terms=()):
        def one(i, carry):
            at = pl.multiple_of(i * step, step)
            total = jnp.dot(
                act_t[rel, pl.ds(row0 + at, step), :],
                cot[:, pl.ds(col0, width)],
                preferred_element_type=jnp.float32,
            )
            for term in terms:
                total = total + term(at).astype(jnp.float32)
            write(at, total)
            return carry

        lax.fori_loop(0, count // step, one, 0)

    counter = Counter()
    sends = []

    def send(src, dst, dev):
        n = counter.take()
        cp = pltpu.make_async_remote_copy(
            src_ref=src,
            dst_ref=dst,
            send_sem=send_sem.at[n],
            recv_sem=recv_sem.at[n],
            device_id=dev,
            device_id_type=MESH,
        )
        cp.start()
        sends.append(cp)
        return cp

    order = ((3, 2, 1, 0), (1, 2, 3, 0))
    ring = {}

    def ring_a(chunk, s, dirs=(0, 1)):
        for dr in dirs:
            col0 = chunk * wide + dr * half_w
            rel = order[dr][s]
            terms = ()
            if s:
                ring[chunk, dr, s - 1].wait_recv()
                terms = (lambda at, dr=dr: ring_recv_a[chunk, dr, s - 1, pl.ds(at, step), :],)
            if s < 3:

                def write(at, total, dr=dr):
                    ring_send_a[chunk, dr, s, pl.ds(at, step), :] = total.astype(jnp.bfloat16)

                product(rel, 0, block, col0, half_w, write, terms)
                ring[chunk, dr, s] = send(
                    ring_send_a.at[chunk, dr, s], ring_recv_a.at[chunk, dr, s], toward[dr]
                )
            else:

                def write_far(at, total, dr=dr):
                    cross_send_a[chunk, pl.ds(at, step), pl.ds(dr * half_w, half_w)] = total.astype(
                        jnp.bfloat16
                    )

                def write_own(at, total, dr=dr):
                    own_a[chunk, pl.ds(at, step), pl.ds(dr * half_w, half_w)] = total

                far = (
                    lambda at, dr=dr: ring_recv_a[chunk, dr, s - 1, pl.ds(at + rows, step), :],
                )
                product(rel, rows, rows, col0, half_w, write_far, far)
                product(rel, 0, rows, col0, half_w, write_own, terms)
        if s == 3:
            ring[chunk, "x"] = send(cross_send_a.at[chunk], cross_recv_a.at[chunk], across)

    def cross_b(dr, s):
        rel = order[dr][s]

        def write(at, total):
            cross_send_b[dr, s, pl.ds(at, step), :] = total.astype(jnp.bfloat16)

        product(rel, rows, rows, 2 * wide + dr * half_w, half_w, write)
        ring["b", "x", dr, s] = send(cross_send_b.at[dr, s], cross_recv_b.at[dr, s], across)

    def ring_b(s):
        for dr in (0, 1):
            ring["b", "x", dr, s].wait_recv()
            terms = [lambda at, dr=dr: cross_recv_b[dr, s, pl.ds(at, step), :]]
            if s:
                ring["b", dr, s - 1].wait_recv()
                terms.append(lambda at, dr=dr: ring_recv_b[dr, s - 1, pl.ds(at, step), :])
            if s < 3:

                def write(at, total, dr=dr):
                    ring_send_b[dr, s, pl.ds(at, step), :] = total.astype(jnp.bfloat16)
            else:

                def write(at, total, dr=dr):
                    own_b[pl.ds(at, step), pl.ds(dr * half_w, half_w)] = total

            product(order[dr][s], 0, rows, 2 * wide + dr * half_w, half_w, write, terms)
            if s < 3:
                ring["b", dr, s] = send(ring_send_b.at[dr, s], ring_recv_b.at[dr, s], toward[dr])

    spreads = {}

    def update(chunk):
        if chunk < 2:
            ring[chunk, "x"].wait_recv()
        cols = pl.ds(chunk * wide, wide)
        few = min(32, rows)

        def one(i, carry):
            at = pl.ds(pl.multiple_of(i * few, few), few)
            if chunk < 2:
                total = own_a[chunk, at, :] + cross_recv_a[chunk, at, :].astype(jnp.float32)
            else:
                total = own_b[at, :]
            new, first, second = adamw(
                total * scale, states[0, at, cols], states[1, at, cols], states[2, at, cols]
            )
            master_out[at, cols] = new
            first_out[at, cols] = first
            second_out[at, cols] = second
            updated_w[chunk, at, :] = new.astype(jnp.bfloat16)
            return carry

        lax.fori_loop(0, rows // few, one, 0)
        spreads[chunk] = [
            send(
                updated_w.at[chunk, pl.ds(pl.multiple_of(slot * piece, piece), piece)],
                spread[chunk].at[me],
                dev,
            )
            for dev, slot in others
        ]
        spread[chunk][me] = updated_w[chunk, pl.ds(pl.multiple_of(me * piece, piece), piece), :]

    moves = {}

    def move(chunk):
        for cp in spreads[chunk]:
            cp.wait_recv()
        cols = pl.ds(chunk * wide, wide)
        for k in range(slots):
            chosen[chunk, k] = spread[chunk][source[k]]
        here = pl.ds(pl.multiple_of(dp_row + me * piece, piece), piece)
        moves[chunk] = [
            send(chosen.at[chunk, slot], weight.at[here, cols], dev) for dev, slot in others
        ]
        weight[here, cols] = chosen[chunk, me]

    gather = {}

    def moved(chunk):
        for cp in moves[chunk]:
            cp.wait_recv()
        here = pl.ds(pl.multiple_of(dp_row, rows), rows)
        cols = pl.ds(chunk * wide, wide)
        if chunk < 2:
            gather[chunk, "x"] = send(weight.at[here, cols], weight.at[here, cols], across)
        else:
            for dr in (0, 1):
                part = pl.ds(chunk * wide + dr * half_w, half_w)
                gather["b", dr, 0] = send(weight.at[here, part], weight.at[here, part], toward[dr])

    def back_b():
        here = pl.ds(pl.multiple_of(dp_row, rows), rows)
        cols = pl.ds(2 * wide, wide)
        gather["b", "x", 0] = send(weight.at[here, cols], weight.at[here, cols], across)

    def gather_a(chunk, s):
        for dr in (0, 1):
            back = (4 - s) if dr == 0 else s
            row0 = pl.multiple_of(lax.rem(z + back, 4) * block, block)
            at = (pl.ds(row0, block), pl.ds(chunk * wide + dr * half_w, half_w))
            if s == 0:
                if dr == 0:
                    gather[chunk, "x"].wait_recv()
            else:
                gather[chunk, dr, s - 1].wait_recv()
            if s < 3:
                gather[chunk, dr, s] = send(weight.at[at], weight.at[at], toward[dr])

    def gather_b(s):
        for dr in (0, 1):
            back = (4 - s) if dr == 0 else s
            row0 = pl.multiple_of((lax.rem(z + back, 4) * 2 + xh) * rows, rows)
            at = (pl.ds(row0, rows), pl.ds(2 * wide + dr * half_w, half_w))
            gather["b", dr, s - 1].wait_recv()
            if s < 3:
                gather["b", dr, s] = send(weight.at[at], weight.at[at], toward[dr])
            gather["b", "x", dr, s] = send(weight.at[at], weight.at[at], across)

    def end_b():
        gather["b", "x", 0].wait_recv()
        for s in (1, 2, 3):
            for dr in (0, 1):
                gather["b", "x", dr, s].wait_recv()

    def find_sources():
        for k in range(slots):
            found = jnp.int32(0)
            for e in range(slots):
                found = jnp.where(new_ref[e] == k, old_ref[e], found)
            source[k] = found

    def enter():
        pl.semaphore_wait(barrier, len(partners))

    def ready():
        for cp in got_states:
            cp.wait()

    plan = (
        (find_sources,),
        (mask_grad, 0),
        (turn, 3),
        (enter,),
        (ring_a, 0, 0, (0,)),
        (turn, 1),
        (ring_a, 0, 0, (1,)),
        (mask_grad, 2),
        (cross_b, 0, 0),
        (cross_b, 1, 0),
        (mask_grad, 1),
        (ring_a, 1, 0),
        (turn, 2),
        (cross_b, 0, 1),
        (cross_b, 1, 1),
        (cross_b, 0, 2),
        (cross_b, 1, 2),
        (ring_a, 0, 1),
        (ring_b, 0),
        (turn, 0),
        (cross_b, 0, 3),
        (cross_b, 1, 3),
        (ring_a, 0, 2),
        (ring_b, 1),
        (ring_a, 1, 1),
        (ring_a, 0, 3),
        (ring_b, 2),
        (ready,),
        (ring_a, 1, 2),
        (update, 0),
        (ring_b, 3),
        (update, 2),
        (move, 0),
        (ring_a, 1, 3),
        (move, 2),
        (moved, 0),
        (moved, 2),
        (back_b,),
        (update, 1),
        (gather_a, 0, 0),
        (gather_b, 1),
        (move, 1),
        (gather_a, 0, 1),
        (gather_b, 2),
        (moved, 1),
        (gather_a, 0, 2),
        (gather_b, 3),
        (gather_a, 1, 0),
        (gather_a, 0, 3),
        (gather_a, 1, 1),
        (gather_a, 1, 2),
        (end_b,),
        (gather_a, 1, 3),
    )
    for task, *given in plan:
        label = "_".join([task.__name__] + [str(g) for g in given])
        with jax.named_scope(label):
            task(*given)
    for cp in sends:
        cp.wait_send()


def solution(mesh):
    finer = Mesh(mesh.devices.reshape(4, 2, 4, 2, 2), AXES)
    return build(finer)


def build(finer):
    ny, nl, nc = (finer.shape[a] for a in EXPERT)
    slots = ny * nl * nc

    def on_device(act, grad, counts, master, moment1, moment2, old_slot, new_slot):
        tokens, width = act.shape[1], act.shape[2]
        columns = grad.shape[2]
        rows = width // 8
        half_w = columns // 6
        wide = 2 * half_w
        block = 2 * rows
        piece = rows // slots
        bf, f32 = jnp.bfloat16, jnp.float32
        sizes = (ny, nl, nc, rows, half_w, tokens, 1.0 / math.sqrt(tokens * 8))
        any_spec = pl.BlockSpec(memory_space=pl.ANY)
        smem = pl.BlockSpec(memory_space=pltpu.SMEM)
        copies = copies_in_all(slots)
        state = pltpu.VMEM((rows, columns), f32)
        new, first, second, moved = pl.pallas_call(
            functools.partial(kernel, sizes),
            out_shape=(state, state, state, pltpu.VMEM((width, columns), bf)),
            in_specs=[smem, smem, smem] + [any_spec] * 5,
            out_specs=(pl.BlockSpec(memory_space=pltpu.VMEM),) * 4,
            scratch_shapes=[
                pltpu.VMEM((4, tokens, block), bf),
                pltpu.VMEM((4, block, tokens), bf),
                pltpu.VMEM((tokens, columns), bf),
                pltpu.VMEM((tokens, columns), bf),
                pltpu.VMEM((3, rows, columns), f32),
                pltpu.VMEM((2, 2, 3, block, half_w), bf),
                pltpu.VMEM((2, 2, 3, block, half_w), bf),
                pltpu.VMEM((2, rows, wide), bf),
                pltpu.VMEM((2, rows, wide), bf),
                pltpu.VMEM((2, rows, wide), f32),
                pltpu.VMEM((2, 4, rows, half_w), bf),
                pltpu.VMEM((2, 4, rows, half_w), bf),
                pltpu.VMEM((2, 3, rows, half_w), bf),
                pltpu.VMEM((2, 3, rows, half_w), bf),
                pltpu.VMEM((rows, wide), f32),
                pltpu.VMEM((3, rows, wide), bf),
                pltpu.VMEM((slots, piece, wide), bf),
                pltpu.VMEM((slots, piece, wide), bf),
                pltpu.VMEM((slots, piece, wide), bf),
                pltpu.VMEM((3, slots, piece, wide), bf),
                pltpu.SMEM((slots,), jnp.int32),
                pltpu.SemaphoreType.DMA((14,)),
                pltpu.SemaphoreType.DMA((copies,)),
                pltpu.SemaphoreType.DMA((copies,)),
            ],
            compiler_params=pltpu.CompilerParams(
                collective_id=0, has_side_effects=True, vmem_limit_bytes=46 << 20
            ),
            name="step",
        )(
            old_slot,
            new_slot,
            counts[0],
            act[0],
            grad[0],
            master[0],
            moment1[0],
            moment2[0],
        )
        return (new[None], first[None], second[None], moved[None])

    in_specs = (
        P(EXPERT, DP, None),
        P(EXPERT, DP, None),
        P(EXPERT, DP),
        P(EXPERT, DP, None),
        P(EXPERT, DP, None),
        P(EXPERT, DP, None),
        P(),
        P(),
    )
    out_specs = (
        P(EXPERT, DP, None),
        P(EXPERT, DP, None),
        P(EXPERT, DP, None),
        P(EXPERT, None, None),
    )
    return jax.shard_map(on_device, mesh=finer, in_specs=in_specs, out_specs=out_specs, check_vma=False)
```

```python
import functools
import math

import jax
import jax.numpy as jnp
from jax import lax
from jax.experimental import pallas as pl
from jax.experimental.pallas import tpu as pltpu
from jax.sharding import Mesh
from jax.sharding import PartitionSpec as P

MESH = pl.DeviceIdType.MESH
AXES = ("z", "xh", "y", "xl", "c")
EXPERT = ("y", "xl", "c")
DP = ("z", "xh")

beta_one = 0.9
beta_two = 0.95
learn_rate = 0.01
decay_rate = 0.1
adam_eps = 1e-08
step_number = 20


def adamw(grads, master, moment1, moment2):
    first = beta_one * moment1 + (1.0 - beta_one) * grads
    second = beta_two * moment2 + (1.0 - beta_two) * grads * grads
    first_hat = first / (1.0 - beta_one**step_number)
    second_hat = second / (1.0 - beta_two**step_number)
    updated = master - learn_rate * (
        first_hat / (jnp.sqrt(second_hat) + adam_eps) + decay_rate * master
    )
    return (updated, first, second)


CHUNKS = (("a", 128), ("a", 128), ("a", 128), ("a", 128), ("b", 256))

PLAN = (
    ("turn", 1),
    ("turn", 2),
    ("turn", 3),
    ("mask", 3),
    ("mask", 0),
    ("find",),
    ("mask", 1),
    ("mask", 4),
    ("enter",),
    ("xb", 4, 0, 1),
    ("ra", 3, 0, 0),
    ("ra", 1, 0, 1),
    ("xb", 4, 0, 2),
    ("xb", 4, 1, 0),
    ("ra", 0, 0, 0),
    ("xb", 4, 0, 0),
    ("ra", 0, 0, 1),
    ("xb", 4, 1, 1),
    ("turn", 0),
    ("ra", 1, 1, 1),
    ("ra", 3, 1, 0),
    ("xb", 4, 1, 3),
    ("ra", 3, 0, 1),
    ("ra", 0, 1, 0),
    ("ra", 0, 1, 1),
    ("ra", 1, 0, 0),
    ("mask", 2),
    ("ra", 3, 1, 1),
    ("ra", 0, 2, 0),
    ("ra", 1, 1, 0),
    ("xb", 4, 1, 2),
    ("ra", 3, 2, 0),
    ("ra", 0, 2, 1),
    ("xb", 4, 0, 3),
    ("ra", 3, 2, 1),
    ("rb", 4, 0, 0),
    ("ra", 1, 2, 1),
    ("ra", 0, 3, 0),
    ("ra", 1, 2, 0),
    ("ra", 0, 3, 1),
    ("ra", 3, 3, 0),
    ("rb", 4, 0, 1),
    ("ra", 3, 3, 1),
    ("up", 0),
    ("ra", 2, 0, 1),
    ("ra", 2, 0, 0),
    ("ra", 1, 3, 1),
    ("rb", 4, 1, 0),
    ("ra", 1, 3, 0),
    ("up", 3),
    ("rb", 4, 1, 1),
    ("mv", 0),
    ("ra", 2, 1, 0),
    ("ra", 2, 1, 1),
    ("up", 1),
    ("rb", 4, 2, 1),
    ("mv", 3),
    ("rb", 4, 2, 0),
    ("md", 0),
    ("ra", 2, 2, 1),
    ("ra", 2, 2, 0),
    ("md", 3),
    ("rb", 4, 3, 0),
    ("rb", 4, 3, 1),
    ("up", 4),
    ("ga", 0, 0, 0),
    ("ga", 0, 0, 1),
    ("ga", 3, 0, 0),
    ("ra", 2, 3, 1),
    ("ga", 3, 0, 1),
    ("mv", 1),
    ("ga", 0, 1, 1),
    ("mv", 4),
    ("ga", 0, 1, 0),
    ("ra", 2, 3, 0),
    ("ga", 3, 1, 0),
    ("ga", 3, 1, 1),
    ("md", 1),
    ("md", 4),
    ("ga", 3, 2, 1),
    ("up", 2),
    ("bx", 4, 0, 1),
    ("ga", 0, 2, 1),
    ("ga", 0, 2, 0),
    ("gb", 4, 1, 1),
    ("ga", 1, 0, 1),
    ("gb", 4, 1, 0),
    ("mv", 2),
    ("bx", 4, 1, 1),
    ("ga", 3, 2, 0),
    ("md", 2),
    ("gb", 4, 2, 0),
    ("ga", 1, 0, 0),
    ("gb", 4, 2, 1),
    ("bx", 4, 2, 1),
    ("ga", 0, 3, 0),
    ("bx", 4, 2, 0),
    ("ga", 2, 0, 0),
    ("bx", 4, 0, 0),
    ("ga", 3, 3, 0),
    ("gb", 4, 3, 0),
    ("ga", 2, 0, 1),
    ("ga", 1, 1, 1),
    ("ga", 1, 1, 0),
    ("ga", 2, 1, 0),
    ("bx", 4, 1, 0),
    ("ga", 2, 1, 1),
    ("ga", 0, 3, 1),
    ("bx", 4, 3, 0),
    ("ga", 1, 2, 0),
    ("ga", 1, 2, 1),
    ("ga", 2, 2, 0),
    ("gb", 4, 3, 1),
    ("bx", 4, 3, 1),
    ("ga", 2, 2, 1),
    ("ga", 3, 3, 1),
    ("ga", 2, 3, 0),
    ("ga", 1, 3, 0),
    ("ga", 1, 3, 1),
    ("ga", 2, 3, 1),
    ("end", 4),
)


class Counter:
    def __init__(self):
        self.used = 0

    def take(self):
        self.used += 1
        return self.used - 1


def copies_in_all(slots):
    moving = 2 * (slots - 1)
    return sum((16 if kind == "a" else 28) + moving for kind, _ in CHUNKS)


def scratch_of(kind, half, rows, slots):
    bf, f32 = jnp.bfloat16, jnp.float32
    block = 2 * rows if kind == "a" else rows
    crossing = 1 if kind == "a" else 4
    return [
        pltpu.VMEM((2, 3, block, half), bf),
        pltpu.VMEM((2, 3, block, half), bf),
        pltpu.VMEM((2, crossing, rows, half), bf),
        pltpu.VMEM((2, crossing, rows, half), bf),
        pltpu.VMEM((2, rows, half), f32),
        pltpu.VMEM((rows, 2 * half), bf),
        pltpu.VMEM((slots, rows // slots, 2 * half), bf),
        pltpu.VMEM((slots, rows // slots, 2 * half), bf),
    ]


PER_CHUNK = 8


def kernel(
    sizes,
    old_ref,
    new_ref,
    count_ref,
    act_hbm,
    grad_hbm,
    master_hbm,
    first_hbm,
    second_hbm,
    master_out,
    first_out,
    second_out,
    weight,
    act_raw,
    act_t,
    grad_raw,
    cot,
    states,
    source,
    load_sem,
    send_sem,
    recv_sem,
    *buffers,
):
    ny, nl, nc, rows, tokens, scale = sizes
    slots = ny * nl * nc
    piece = rows // slots
    block = 2 * rows
    z, xh, y, xl, c = (lax.axis_index(a) for a in AXES)
    me = (y * nl + xl) * nc + c
    dp_row = (z * 2 + xh) * rows
    step = min(256, rows)

    kinds, halves, starts, parts = [], [], [], []
    at_column = 0
    for k, (kind, half) in enumerate(CHUNKS):
        kinds.append(kind)
        halves.append(half)
        starts.append(at_column)
        parts.append(buffers[k * PER_CHUNK : (k + 1) * PER_CHUNK])
        at_column += 2 * half
    ring_send, ring_recv, cross_send, cross_recv, own, updated, spread, chosen = zip(*parts)

    def columns(k, dr):
        return pl.ds(starts[k] + dr * halves[k], halves[k])

    def both(k):
        return pl.ds(starts[k], 2 * halves[k])

    def device(zz=None, xx=None, slot=None):
        yy, ll, cc = slot if slot is not None else (y, xl, c)
        return (z if zz is None else zz, xh if xx is None else xx, yy, ll, cc)

    z_next = lax.rem(z + 1, 4)
    z_prev = lax.rem(z + 3, 4)
    toward = (device(zz=z_next), device(zz=z_prev))
    across = device(xx=1 - xh)
    others = []
    for jy in range(ny):
        for jl in range(nl):
            for jc in range(nc):
                if jy or jl or jc:
                    slot = (lax.rem(y + jy, ny), lax.rem(xl + jl, nl), lax.rem(c + jc, nc))
                    others.append((device(slot=slot), (slot[0] * nl + slot[1]) * nc + slot[2]))

    loads = []

    def load(src, dst):
        cp = pltpu.make_async_copy(src, dst, load_sem.at[len(loads)])
        cp.start()
        loads.append(cp)
        return cp

    got = {}
    for name, *given in PLAN:
        if name == "mask":
            cols = both(given[0])
            got[name, given[0]] = [load(grad_hbm.at[:, cols], grad_raw.at[:, cols])]
        if name == "turn":
            rel = given[0]
            base = lax.rem(z + rel, 4) * block
            got[name, rel] = []
            for part, at in ((0, xh), (1, 1 - xh)):
                cols = pl.ds(pl.multiple_of(base + at * rows, rows), rows)
                got[name, rel].append(
                    load(act_hbm.at[:, cols], act_raw.at[rel, :, pl.ds(part * rows, rows)])
                )
    got["states"] = [
        load(ref, states.at[n]) for n, ref in enumerate((master_hbm, first_hbm, second_hbm))
    ]

    def loaded(*key):
        for cp in got.pop(key if len(key) > 1 else key[0], ()):
            cp.wait()

    barrier = pltpu.get_barrier_semaphore()
    partners = [toward[0], toward[1], across] + [dev for dev, _ in others]
    for dev in partners:
        pl.semaphore_signal(barrier, inc=1, device_id=dev, device_id_type=MESH)

    live = count_ref[0]

    def find():
        for k in range(slots):
            found = jnp.int32(0)
            for e in range(slots):
                found = jnp.where(new_ref[e] == k, old_ref[e], found)
            source[k] = found

    def enter():
        pl.semaphore_wait(barrier, len(partners))

    def mask(k):
        loaded("mask", k)
        keep = lax.broadcasted_iota(jnp.int32, (tokens, 128), 0) < live
        for j in range(2 * halves[k] // 128):
            cols = pl.ds(starts[k] + j * 128, 128)
            part = grad_raw[:, cols]
            cot[:, cols] = jnp.where(keep, part, jnp.zeros_like(part))

    def turn(rel):
        loaded("turn", rel)

        def one(i, carry):
            at = pl.ds(pl.multiple_of(i * 128, 128), 128)
            act_t[rel, at, :] = act_raw[rel, :, at].T
            return carry

        lax.fori_loop(0, block // 128, one, 0)

    def product(rel, row0, count, cols, write, terms=()):
        def one(i, carry):
            at = pl.multiple_of(i * step, step)
            total = jnp.dot(
                act_t[rel, pl.ds(row0 + at, step), :],
                cot[:, cols],
                preferred_element_type=jnp.float32,
            )
            for ref, first in terms:
                total = total + ref[pl.ds(at + first, step), :].astype(jnp.float32)
            write[pl.ds(at, step), :] = total.astype(write.dtype)
            return carry

        lax.fori_loop(0, count // step, one, 0)

    counter = Counter()
    sends = []
    sent = {}

    def send(src, dst, dev):
        n = counter.take()
        cp = pltpu.make_async_remote_copy(
            src_ref=src,
            dst_ref=dst,
            send_sem=send_sem.at[n],
            recv_sem=recv_sem.at[n],
            device_id=dev,
            device_id_type=MESH,
        )
        cp.start()
        sends.append(cp)
        return cp

    order = ((3, 2, 1, 0), (1, 2, 3, 0))

    def ra(k, s, dr):
        rel, cols = order[dr][s], columns(k, dr)
        if s:
            sent["z", k, dr, s - 1].wait_recv()
            before = ring_recv[k].at[dr, s - 1]
        if s < 3:
            dst = ring_send[k].at[dr, s]
            product(rel, 0, block, cols, dst, ((before, 0),) if s else ())
            sent["z", k, dr, s] = send(dst, ring_recv[k].at[dr, s], toward[dr])
        else:
            far = cross_send[k].at[dr, 0]
            product(rel, rows, rows, cols, far, ((before, rows),))
            sent["x", k, dr] = send(far, cross_recv[k].at[dr, 0], across)
            product(rel, 0, rows, cols, own[k].at[dr], ((before, 0),))

    def xb(k, dr, s):
        far = cross_send[k].at[dr, s]
        product(order[dr][s], rows, rows, columns(k, dr), far)
        sent["x", k, dr, s] = send(far, cross_recv[k].at[dr, s], across)

    def rb(k, s, dr):
        sent["x", k, dr, s].wait_recv()
        terms = [(cross_recv[k].at[dr, s], 0)]
        if s:
            sent["z", k, dr, s - 1].wait_recv()
            terms.append((ring_recv[k].at[dr, s - 1], 0))
        dst = ring_send[k].at[dr, s] if s < 3 else own[k].at[dr]
        product(order[dr][s], 0, rows, columns(k, dr), dst, terms)
        if s < 3:
            sent["z", k, dr, s] = send(dst, ring_recv[k].at[dr, s], toward[dr])

    def up(k):
        loaded("states")
        half = halves[k]
        few = min(rows, 32 * 256 // half)
        for dr in (0, 1):
            if kinds[k] == "a":
                sent["x", k, dr].wait_recv()
            cols = columns(k, dr)

            def one(i, carry, dr=dr, cols=cols):
                at = pl.ds(pl.multiple_of(i * few, few), few)
                total = own[k][dr, at, :]
                if kinds[k] == "a":
                    total = total + cross_recv[k][dr, 0, at, :].astype(jnp.float32)
                new, first, second = adamw(
                    total * scale, states[0, at, cols], states[1, at, cols], states[2, at, cols]
                )
                master_out[at, cols] = new
                first_out[at, cols] = first
                second_out[at, cols] = second
                updated[k][at, pl.ds(dr * half, half)] = new.astype(jnp.bfloat16)
                return carry

            lax.fori_loop(0, rows // few, one, 0)
        sent["spread", k] = [
            send(
                updated[k].at[pl.ds(pl.multiple_of(slot * piece, piece), piece)],
                spread[k].at[me],
                dev,
            )
            for dev, slot in others
        ]
        spread[k][me] = updated[k][pl.ds(pl.multiple_of(me * piece, piece), piece), :]

    def mv(k):
        for cp in sent["spread", k]:
            cp.wait_recv()
        for slot in range(slots):
            chosen[k][slot] = spread[k][source[slot]]
        here = (pl.ds(pl.multiple_of(dp_row + me * piece, piece), piece), both(k))
        sent["move", k] = [send(chosen[k].at[slot], weight.at[here], dev) for dev, slot in others]
        weight[here] = chosen[k][me]

    def pass_on(at, dev):
        return send(weight.at[at], weight.at[at], dev)

    def md(k):
        for cp in sent["move", k]:
            cp.wait_recv()
        here = pl.ds(pl.multiple_of(dp_row, rows), rows)
        for dr in (0, 1):
            at = (here, columns(k, dr))
            if kinds[k] == "a":
                sent["gx", k, dr] = pass_on(at, across)
            else:
                sent["gz", k, dr, 0] = pass_on(at, toward[dr])

    def z_block(s, dr):
        return lax.rem(z + ((4 - s) if dr == 0 else s), 4)

    def ga(k, s, dr):
        row0 = pl.multiple_of(z_block(s, dr) * block, block)
        if s:
            sent["gz", k, dr, s - 1].wait_recv()
        else:
            sent["gx", k, dr].wait_recv()
        if s < 3:
            sent["gz", k, dr, s] = pass_on((pl.ds(row0, block), columns(k, dr)), toward[dr])

    def b_rows(k, s, dr):
        row0 = pl.multiple_of((z_block(s, dr) * 2 + xh) * rows, rows)
        return (pl.ds(row0, rows), columns(k, dr))

    def gb(k, s, dr):
        sent["gz", k, dr, s - 1].wait_recv()
        if s < 3:
            sent["gz", k, dr, s] = pass_on(b_rows(k, s, dr), toward[dr])

    def bx(k, s, dr):
        sent["bx", k, dr, s] = pass_on(b_rows(k, s, dr), across)

    def end(k):
        for dr in (0, 1):
            for s in range(4):
                sent["bx", k, dr, s].wait_recv()

    tasks = (find, enter, mask, turn, ra, xb, rb, up, mv, md, ga, gb, bx, end)
    named = {task.__name__: task for task in tasks}
    for name, *given in PLAN:
        with jax.named_scope("_".join([name] + [str(g) for g in given])):
            named[name](*given)
    for cp in sends:
        cp.wait_send()


def solution(mesh):
    finer = Mesh(mesh.devices.reshape(4, 2, 4, 2, 2), AXES)
    return build(finer)


def build(finer):
    ny, nl, nc = (finer.shape[a] for a in EXPERT)
    slots = ny * nl * nc

    def on_device(act, grad, counts, master, moment1, moment2, old_slot, new_slot):
        tokens, width = act.shape[1], act.shape[2]
        columns = grad.shape[2]
        rows = width // 8
        block = 2 * rows
        bf, f32 = jnp.bfloat16, jnp.float32
        sizes = (ny, nl, nc, rows, tokens, 1.0 / math.sqrt(tokens * 8))
        any_spec = pl.BlockSpec(memory_space=pl.ANY)
        smem = pl.BlockSpec(memory_space=pltpu.SMEM)
        copies = copies_in_all(slots)
        state = pltpu.VMEM((rows, columns), f32)
        scratch = [
            pltpu.VMEM((4, tokens, block), bf),
            pltpu.VMEM((4, block, tokens), bf),
            pltpu.VMEM((tokens, columns), bf),
            pltpu.VMEM((tokens, columns), bf),
            pltpu.VMEM((3, rows, columns), f32),
            pltpu.SMEM((slots,), jnp.int32),
            pltpu.SemaphoreType.DMA((len(CHUNKS) + 11,)),
            pltpu.SemaphoreType.DMA((copies,)),
            pltpu.SemaphoreType.DMA((copies,)),
        ]
        for kind, half in CHUNKS:
            scratch += scratch_of(kind, half, rows, slots)
        new, first, second, moved = pl.pallas_call(
            functools.partial(kernel, sizes),
            out_shape=(state, state, state, pltpu.VMEM((width, columns), bf)),
            in_specs=[smem, smem, smem] + [any_spec] * 5,
            out_specs=(pl.BlockSpec(memory_space=pltpu.VMEM),) * 4,
            scratch_shapes=scratch,
            compiler_params=pltpu.CompilerParams(
                collective_id=0, has_side_effects=True, vmem_limit_bytes=46 << 20
            ),
            name="step",
        )(
            old_slot,
            new_slot,
            counts[0],
            act[0],
            grad[0],
            master[0],
            moment1[0],
            moment2[0],
        )
        return (new[None], first[None], second[None], moved[None])

    in_specs = (
        P(EXPERT, DP, None),
        P(EXPERT, DP, None),
        P(EXPERT, DP),
        P(EXPERT, DP, None),
        P(EXPERT, DP, None),
        P(EXPERT, DP, None),
        P(),
        P(),
    )
    out_specs = (
        P(EXPERT, DP, None),
        P(EXPERT, DP, None),
        P(EXPERT, DP, None),
        P(EXPERT, None, None),
    )
    return jax.shard_map(on_device, mesh=finer, in_specs=in_specs, out_specs=out_specs, check_vma=False)
```

```python
import functools
import math

import jax
import jax.numpy as jnp
from jax import lax
from jax.experimental import pallas as pl
from jax.experimental.pallas import tpu as pltpu
from jax.sharding import Mesh
from jax.sharding import PartitionSpec as P

MESH = pl.DeviceIdType.MESH
AXES = ("z", "xh", "y", "xl", "c")
EXPERT = ("y", "xl", "c")
DP = ("z", "xh")

beta_one = 0.9
beta_two = 0.95
learn_rate = 0.01
decay_rate = 0.1
adam_eps = 1e-08
step_number = 20


def adamw(grads, master, moment1, moment2):
    first = beta_one * moment1 + (1.0 - beta_one) * grads
    second = beta_two * moment2 + (1.0 - beta_two) * grads * grads
    first_hat = first / (1.0 - beta_one**step_number)
    second_hat = second / (1.0 - beta_two**step_number)
    updated = master - learn_rate * (
        first_hat / (jnp.sqrt(second_hat) + adam_eps) + decay_rate * master
    )
    return (updated, first, second)


CHUNKS = (("a", 128), ("a", 128), ("a", 128), ("a", 128), ("b", 256))

PLAN = (
    ("find",),
    ("mask", 0),
    ("turn", 1),
    ("mask", 4),
    ("enter",),
    ("xb", 4, 0, 2),
    ("ra", 0, 0, 1),
    ("turn", 3),
    ("ra", 0, 0, 0),
    ("xb", 4, 1, 0),
    ("mask", 1),
    ("ra", 1, 0, 1),
    ("ra", 1, 0, 0),
    ("xb", 4, 1, 2),
    ("turn", 2),
    ("ra", 0, 1, 1),
    ("turn", 0),
    ("ra", 0, 1, 0),
    ("xb", 4, 0, 0),
    ("ra", 1, 1, 1),
    ("xb", 4, 1, 1),
    ("ra", 1, 1, 0),
    ("xb", 4, 0, 1),
    ("ra", 0, 2, 1),
    ("ra", 0, 2, 0),
    ("rb", 4, 0, 1),
    ("rb", 4, 0, 0),
    ("ra", 1, 2, 1),
    ("ra", 1, 2, 0),
    ("ra", 0, 3, 1),
    ("mask", 2),
    ("ra", 0, 3, 0),
    ("xb", 4, 0, 3),
    ("rb", 4, 1, 1),
    ("ra", 2, 0, 1),
    ("rb", 4, 1, 0),
    ("ra", 2, 0, 0),
    ("ra", 1, 3, 1),
    ("ra", 1, 3, 0),
    ("up", 0),
    ("xb", 4, 1, 3),
    ("rb", 4, 2, 0),
    ("mask", 3),
    ("rb", 4, 2, 1),
    ("ra", 3, 0, 0),
    ("up", 1),
    ("ra", 3, 0, 1),
    ("ra", 2, 1, 0),
    ("mv", 0),
    ("ra", 2, 1, 1),
    ("rb", 4, 3, 0),
    ("rb", 4, 3, 1),
    ("up", 4),
    ("ra", 3, 1, 0),
    ("ra", 3, 1, 1),
    ("md", 0),
    ("ra", 2, 2, 0),
    ("ra", 2, 2, 1),
    ("mv", 1),
    ("ra", 3, 2, 0),
    ("mv", 4),
    ("ra", 3, 2, 1),
    ("ra", 2, 3, 0),
    ("ra", 2, 3, 1),
    ("ga", 0, 0, 0),
    ("ga", 0, 0, 1),
    ("md", 1),
    ("ra", 3, 3, 0),
    ("md", 4),
    ("ra", 3, 3, 1),
    ("ga", 0, 1, 0),
    ("ga", 0, 1, 1),
    ("up", 2),
    ("gb", 4, 1, 1),
    ("bx", 4, 1, 1),
    ("ga", 1, 0, 0),
    ("gb", 4, 1, 0),
    ("up", 3),
    ("ga", 0, 2, 0),
    ("ga", 1, 0, 1),
    ("mv", 2),
    ("gb", 4, 2, 1),
    ("bx", 4, 2, 1),
    ("ga", 1, 1, 1),
    ("ga", 1, 1, 0),
    ("mv", 3),
    ("md", 2),
    ("ga", 0, 2, 1),
    ("gb", 4, 3, 1),
    ("gb", 4, 2, 0),
    ("md", 3),
    ("bx", 4, 2, 0),
    ("ga", 1, 2, 0),
    ("ga", 1, 2, 1),
    ("ga", 2, 0, 0),
    ("gb", 4, 3, 0),
    ("ga", 2, 0, 1),
    ("bx", 4, 1, 0),
    ("ga", 3, 0, 1),
    ("bx", 4, 3, 1),
    ("ga", 3, 0, 0),
    ("bx", 4, 0, 1),
    ("ga", 2, 1, 1),
    ("ga", 2, 1, 0),
    ("ga", 3, 1, 0),
    ("ga", 3, 1, 1),
    ("bx", 4, 0, 0),
    ("bx", 4, 3, 0),
    ("ga", 0, 3, 0),
    ("ga", 2, 2, 1),
    ("ga", 2, 2, 0),
    ("ga", 3, 2, 1),
    ("ga", 0, 3, 1),
    ("ga", 1, 3, 1),
    ("ga", 3, 2, 0),
    ("ga", 3, 3, 0),
    ("ga", 1, 3, 0),
    ("ga", 3, 3, 1),
    ("ga", 2, 3, 1),
    ("ga", 2, 3, 0),
    ("end", 4),
)


class Counter:
    def __init__(self):
        self.used = 0

    def take(self):
        self.used += 1
        return self.used - 1


def semaphores_in_all():
    return sum(18 if kind == "a" else 30 for kind, _ in CHUNKS)


def scratch_of(kind, half, rows, slots):
    bf, f32 = jnp.bfloat16, jnp.float32
    block = 2 * rows if kind == "a" else rows
    crossing = 1 if kind == "a" else 4
    return [
        pltpu.VMEM((2, 3, block, half), bf),
        pltpu.VMEM((2, 3, block, half), bf),
        pltpu.VMEM((2, crossing, rows, half), bf),
        pltpu.VMEM((2, crossing, rows, half), bf),
        pltpu.VMEM((2, rows, half), f32),
        pltpu.VMEM((rows, 2 * half), bf),
        pltpu.VMEM((slots, rows // slots, 2 * half), bf),
        pltpu.VMEM((slots, rows // slots, 2 * half), bf),
    ]


PER_CHUNK = 8


def kernel(
    sizes,
    old_ref,
    new_ref,
    count_ref,
    act_hbm,
    grad_hbm,
    master_hbm,
    first_hbm,
    second_hbm,
    master_out,
    first_out,
    second_out,
    weight,
    act_raw,
    act_t,
    grad_raw,
    cot,
    states,
    source,
    load_sem,
    send_sem,
    recv_sem,
    *buffers,
):
    ny, nl, nc, rows, tokens, scale = sizes
    slots = ny * nl * nc
    piece = rows // slots
    block = 2 * rows
    z, xh, y, xl, c = (lax.axis_index(a) for a in AXES)
    me = (y * nl + xl) * nc + c
    dp_row = (z * 2 + xh) * rows

    kinds, halves, starts, parts = [], [], [], []
    at_column = 0
    for k, (kind, half) in enumerate(CHUNKS):
        kinds.append(kind)
        halves.append(half)
        starts.append(at_column)
        parts.append(buffers[k * PER_CHUNK : (k + 1) * PER_CHUNK])
        at_column += 2 * half
    ring_send, ring_recv, cross_send, cross_recv, own, updated, spread, chosen = zip(*parts)

    def columns(k, dr):
        return pl.ds(starts[k] + dr * halves[k], halves[k])

    def both(k):
        return pl.ds(starts[k], 2 * halves[k])

    def device(zz=None, xx=None, slot=None):
        yy, ll, cc = slot if slot is not None else (y, xl, c)
        return (z if zz is None else zz, xh if xx is None else xx, yy, ll, cc)

    z_next = lax.rem(z + 1, 4)
    z_prev = lax.rem(z + 3, 4)
    toward = (device(zz=z_next), device(zz=z_prev))
    across = device(xx=1 - xh)
    others = []
    for jy in range(ny):
        for jl in range(nl):
            for jc in range(nc):
                if jy or jl or jc:
                    slot = (lax.rem(y + jy, ny), lax.rem(xl + jl, nl), lax.rem(c + jc, nc))
                    others.append((device(slot=slot), (slot[0] * nl + slot[1]) * nc + slot[2]))

    loads = []

    def load(src, dst):
        cp = pltpu.make_async_copy(src, dst, load_sem.at[len(loads)])
        cp.start()
        loads.append(cp)
        return cp

    got = {}
    for name, *given in PLAN:
        if name == "mask":
            cols = both(given[0])
            got[name, given[0]] = [load(grad_hbm.at[:, cols], grad_raw.at[:, cols])]
        if name == "turn":
            rel = given[0]
            base = lax.rem(z + rel, 4) * block
            got[name, rel] = []
            for part, at in ((0, xh), (1, 1 - xh)):
                cols = pl.ds(pl.multiple_of(base + at * rows, rows), rows)
                got[name, rel].append(
                    load(act_hbm.at[:, cols], act_raw.at[rel, :, pl.ds(part * rows, rows)])
                )
    got["states"] = [
        load(ref, states.at[n]) for n, ref in enumerate((master_hbm, first_hbm, second_hbm))
    ]

    def loaded(*key):
        for cp in got.pop(key if len(key) > 1 else key[0], ()):
            cp.wait()

    barrier = pltpu.get_barrier_semaphore()
    partners = [toward[0], toward[1], across] + [dev for dev, _ in others]
    for dev in partners:
        pl.semaphore_signal(barrier, inc=1, device_id=dev, device_id_type=MESH)

    live = count_ref[0]

    def find():
        for k in range(slots):
            found = jnp.int32(0)
            for e in range(slots):
                found = jnp.where(new_ref[e] == k, old_ref[e], found)
            source[k] = found

    def enter():
        pl.semaphore_wait(barrier, len(partners))

    def mask(k):
        loaded("mask", k)
        keep = lax.broadcasted_iota(jnp.int32, (tokens, 128), 0) < live
        for j in range(2 * halves[k] // 128):
            cols = pl.ds(starts[k] + j * 128, 128)
            part = grad_raw[:, cols]
            cot[:, cols] = jnp.where(keep, part, jnp.zeros_like(part))

    def turn(rel):
        loaded("turn", rel)

        def one(i, carry):
            at = pl.ds(pl.multiple_of(i * 128, 128), 128)
            act_t[rel, at, :] = act_raw[rel, :, at].T
            return carry

        lax.fori_loop(0, block // 128, one, 0)

    def product(rel, row0, count, cols, write, terms=()):
        step = min(count, 256)

        def one(i, carry):
            at = pl.multiple_of(i * step, step)
            total = jnp.dot(
                act_t[rel, pl.ds(row0 + at, step), :],
                cot[:, cols],
                preferred_element_type=jnp.float32,
            )
            for ref, first in terms:
                total = total + ref[pl.ds(at + first, step), :].astype(jnp.float32)
            write[pl.ds(at, step), :] = total.astype(write.dtype)
            return carry

        lax.fori_loop(0, count // step, one, 0)

    counter = Counter()
    sends = []
    sent = {}

    def copy_of(src, dst, dev, n):
        return pltpu.make_async_remote_copy(
            src_ref=src,
            dst_ref=dst,
            send_sem=send_sem.at[n],
            recv_sem=recv_sem.at[n],
            device_id=dev,
            device_id_type=MESH,
        )

    def send(src, dst, dev):
        cp = copy_of(src, dst, dev, counter.take())
        cp.start()
        sends.append(cp)
        return cp

    def send_group(pairs, pieces):
        n = counter.take()
        for src, dst, dev in pairs:
            copy_of(src, dst, dev, n).start()
        whole = pieces.at[pl.ds(0, slots - 1)]
        cp = copy_of(whole, whole, across, n)
        sends.append(cp)
        return cp

    order = ((3, 2, 1, 0), (1, 2, 3, 0))

    def ra(k, s, dr):
        rel, cols = order[dr][s], columns(k, dr)
        if s:
            sent["z", k, dr, s - 1].wait_recv()
            before = ring_recv[k].at[dr, s - 1]
        if s < 3:
            dst = ring_send[k].at[dr, s]
            product(rel, 0, block, cols, dst, ((before, 0),) if s else ())
            sent["z", k, dr, s] = send(dst, ring_recv[k].at[dr, s], toward[dr])
        else:
            far = cross_send[k].at[dr, 0]
            product(rel, rows, rows, cols, far, ((before, rows),))
            sent["x", k, dr] = send(far, cross_recv[k].at[dr, 0], across)
            product(rel, 0, rows, cols, own[k].at[dr], ((before, 0),))

    def xb(k, dr, s):
        far = cross_send[k].at[dr, s]
        product(order[dr][s], rows, rows, columns(k, dr), far)
        sent["x", k, dr, s] = send(far, cross_recv[k].at[dr, s], across)

    def rb(k, s, dr):
        sent["x", k, dr, s].wait_recv()
        terms = [(cross_recv[k].at[dr, s], 0)]
        if s:
            sent["z", k, dr, s - 1].wait_recv()
            terms.append((ring_recv[k].at[dr, s - 1], 0))
        dst = ring_send[k].at[dr, s] if s < 3 else own[k].at[dr]
        product(order[dr][s], 0, rows, columns(k, dr), dst, terms)
        if s < 3:
            sent["z", k, dr, s] = send(dst, ring_recv[k].at[dr, s], toward[dr])

    def up(k):
        loaded("states")
        half = halves[k]
        few = min(rows, 32 * 256 // half)
        for dr in (0, 1):
            if kinds[k] == "a":
                sent["x", k, dr].wait_recv()
            cols = columns(k, dr)

            def one(i, carry, dr=dr, cols=cols):
                at = pl.ds(pl.multiple_of(i * few, few), few)
                total = own[k][dr, at, :]
                if kinds[k] == "a":
                    total = total + cross_recv[k][dr, 0, at, :].astype(jnp.float32)
                new, first, second = adamw(
                    total * scale, states[0, at, cols], states[1, at, cols], states[2, at, cols]
                )
                master_out[at, cols] = new
                first_out[at, cols] = first
                second_out[at, cols] = second
                updated[k][at, pl.ds(dr * half, half)] = new.astype(jnp.bfloat16)
                return carry

            lax.fori_loop(0, rows // few, one, 0)
        sent["spread", k] = send_group(
            [
                (
                    updated[k].at[pl.ds(pl.multiple_of(slot * piece, piece), piece)],
                    spread[k].at[me],
                    dev,
                )
                for dev, slot in others
            ],
            spread[k],
        )
        spread[k][me] = updated[k][pl.ds(pl.multiple_of(me * piece, piece), piece), :]

    def mv(k):
        sent["spread", k].wait_recv()
        for slot in range(slots):
            chosen[k][slot] = spread[k][source[slot]]
        here = (pl.ds(pl.multiple_of(dp_row + me * piece, piece), piece), both(k))
        sent["move", k] = send_group(
            [(chosen[k].at[slot], weight.at[here], dev) for dev, slot in others], chosen[k]
        )
        weight[here] = chosen[k][me]

    def pass_on(at, dev):
        return send(weight.at[at], weight.at[at], dev)

    def md(k):
        sent["move", k].wait_recv()
        here = pl.ds(pl.multiple_of(dp_row, rows), rows)
        for dr in (0, 1):
            at = (here, columns(k, dr))
            if kinds[k] == "a":
                sent["gx", k, dr] = pass_on(at, across)
            else:
                sent["gz", k, dr, 0] = pass_on(at, toward[dr])

    def z_block(s, dr):
        return lax.rem(z + ((4 - s) if dr == 0 else s), 4)

    def ga(k, s, dr):
        row0 = pl.multiple_of(z_block(s, dr) * block, block)
        if s:
            sent["gz", k, dr, s - 1].wait_recv()
        else:
            sent["gx", k, dr].wait_recv()
        if s < 3:
            sent["gz", k, dr, s] = pass_on((pl.ds(row0, block), columns(k, dr)), toward[dr])

    def b_rows(k, s, dr):
        row0 = pl.multiple_of((z_block(s, dr) * 2 + xh) * rows, rows)
        return (pl.ds(row0, rows), columns(k, dr))

    def gb(k, s, dr):
        sent["gz", k, dr, s - 1].wait_recv()
        if s < 3:
            sent["gz", k, dr, s] = pass_on(b_rows(k, s, dr), toward[dr])

    def bx(k, s, dr):
        sent["bx", k, dr, s] = pass_on(b_rows(k, s, dr), across)

    def end(k):
        for dr in (0, 1):
            for s in range(4):
                sent["bx", k, dr, s].wait_recv()

    tasks = (find, enter, mask, turn, ra, xb, rb, up, mv, md, ga, gb, bx, end)
    named = {task.__name__: task for task in tasks}
    ended, issued = 0, []
    for name, *given in PLAN:
        with jax.named_scope("_".join([name] + [str(g) for g in given])):
            if name in ("ga", "gb", "md") and len(issued) > 20:
                until = min(issued[-20], ended + 9)
                for cp in sends[ended:until]:
                    cp.wait_send()
                ended = max(ended, until)
            named[name](*given)
        issued.append(len(sends))
    with jax.named_scope("rest"):
        for cp in sends[ended:]:
            cp.wait_send()


def keep(*refs):
    sem = refs[8]
    copies = []
    for src, dst in zip(refs[:4], refs[4:8]):
        half = src.shape[0] // 2
        for row0 in (0, half):
            at = pl.ds(row0, half)
            copies.append(pltpu.make_async_copy(src.at[at], dst.at[at], sem.at[len(copies)]))
    for cp in copies:
        cp.start()
    for cp in copies:
        cp.wait()


def solution(mesh):
    finer = Mesh(mesh.devices.reshape(4, 2, 4, 2, 2), AXES)
    return build(finer)


def build(finer):
    ny, nl, nc = (finer.shape[a] for a in EXPERT)
    slots = ny * nl * nc

    def on_device(act, grad, counts, master, moment1, moment2, old_slot, new_slot):
        tokens, width = act.shape[1], act.shape[2]
        columns = grad.shape[2]
        rows = width // 8
        block = 2 * rows
        bf, f32 = jnp.bfloat16, jnp.float32
        sizes = (ny, nl, nc, rows, tokens, 1.0 / math.sqrt(tokens * 8))
        any_spec = pl.BlockSpec(memory_space=pl.ANY)
        smem = pl.BlockSpec(memory_space=pltpu.SMEM)
        copies = semaphores_in_all()
        state = pltpu.VMEM((rows, columns), f32)
        scratch = [
            pltpu.VMEM((4, tokens, block), bf),
            pltpu.VMEM((4, block, tokens), bf),
            pltpu.VMEM((tokens, columns), bf),
            pltpu.VMEM((tokens, columns), bf),
            pltpu.VMEM((3, rows, columns), f32),
            pltpu.SMEM((slots,), jnp.int32),
            pltpu.SemaphoreType.DMA((len(CHUNKS) + 11,)),
            pltpu.SemaphoreType.DMA((copies,)),
            pltpu.SemaphoreType.DMA((copies,)),
        ]
        for kind, half in CHUNKS:
            scratch += scratch_of(kind, half, rows, slots)
        results = pl.pallas_call(
            functools.partial(kernel, sizes),
            out_shape=(state, state, state, pltpu.VMEM((width, columns), bf)),
            in_specs=[smem, smem, smem] + [any_spec] * 5,
            out_specs=(pl.BlockSpec(memory_space=pltpu.VMEM),) * 4,
            scratch_shapes=scratch,
            compiler_params=pltpu.CompilerParams(
                collective_id=0, has_side_effects=True, vmem_limit_bytes=46 << 20
            ),
            name="step",
        )(
            old_slot,
            new_slot,
            counts[0],
            act[0],
            grad[0],
            master[0],
            moment1[0],
            moment2[0],
        )
        new, first, second, moved = pl.pallas_call(
            keep,
            out_shape=tuple(jax.ShapeDtypeStruct(r.shape, r.dtype) for r in results),
            in_specs=[pl.BlockSpec(memory_space=pltpu.VMEM)] * 4,
            out_specs=(any_spec,) * 4,
            scratch_shapes=[pltpu.SemaphoreType.DMA((8,))],
            compiler_params=pltpu.CompilerParams(vmem_limit_bytes=1 << 20),
            name="keep",
        )(*results)
        return (new[None], first[None], second[None], moved[None])

    in_specs = (
        P(EXPERT, DP, None),
        P(EXPERT, DP, None),
        P(EXPERT, DP),
        P(EXPERT, DP, None),
        P(EXPERT, DP, None),
        P(EXPERT, DP, None),
        P(),
        P(),
    )
    out_specs = (
        P(EXPERT, DP, None),
        P(EXPERT, DP, None),
        P(EXPERT, DP, None),
        P(EXPERT, None, None),
    )
    return jax.shard_map(on_device, mesh=finer, in_specs=in_specs, out_specs=out_specs, check_vma=False)
```

```python
import functools
import math

import jax
import jax.numpy as jnp
from jax import lax
from jax.experimental import pallas as pl
from jax.experimental.pallas import tpu as pltpu
from jax.sharding import Mesh
from jax.sharding import PartitionSpec as P

MESH = pl.DeviceIdType.MESH
AXES = ("z", "xh", "y", "xl", "c")
EXPERT = ("y", "xl", "c")
DP = ("z", "xh")

beta_one = 0.9
beta_two = 0.95
learn_rate = 0.01
decay_rate = 0.1
adam_eps = 1e-08
step_number = 20


def adamw(grads, master, moment1, moment2):
    first = beta_one * moment1 + (1.0 - beta_one) * grads
    second = beta_two * moment2 + (1.0 - beta_two) * grads * grads
    first_hat = first / (1.0 - beta_one**step_number)
    second_hat = second / (1.0 - beta_two**step_number)
    updated = master - learn_rate * (
        first_hat / (jnp.sqrt(second_hat) + adam_eps) + decay_rate * master
    )
    return (updated, first, second)


CHUNKS = (("a", 128), ("a", 128), ("a", 128), ("a", 128), ("b", 256))

PLAN = (
    ("turn", 3),
    ("mask", 4),
    ("enter",),
    ("xb", 4, 0, 0),
    ("mask", 3),
    ("turn", 1),
    ("ra", 3, 0, 1),
    ("ra", 3, 0, 0),
    ("xb", 4, 1, 0),
    ("mask", 1),
    ("ra", 1, 0, 1),
    ("ra", 1, 0, 0),
    ("xb", 4, 1, 2),
    ("turn", 2),
    ("xb", 4, 1, 1),
    ("ra", 3, 1, 1),
    ("ra", 3, 1, 0),
    ("turn", 0),
    ("rb", 4, 0, 1),
    ("xb", 4, 0, 1),
    ("find",),
    ("rb", 4, 0, 0),
    ("xb", 4, 1, 3),
    ("ra", 3, 2, 1),
    ("ra", 3, 2, 0),
    ("mask", 2),
    ("ra", 1, 1, 1),
    ("ra", 1, 1, 0),
    ("xb", 4, 0, 2),
    ("rb", 4, 1, 1),
    ("rb", 4, 1, 0),
    ("mask", 0),
    ("ra", 3, 3, 1),
    ("ra", 3, 3, 0),
    ("ra", 2, 0, 1),
    ("ra", 1, 2, 1),
    ("ra", 1, 2, 0),
    ("xb", 4, 0, 3),
    ("rb", 4, 2, 1),
    ("ra", 0, 0, 1),
    ("rb", 4, 2, 0),
    ("up", 3),
    ("ra", 2, 1, 1),
    ("ra", 0, 0, 0),
    ("ra", 1, 3, 0),
    ("ra", 1, 3, 1),
    ("ra", 2, 0, 0),
    ("rb", 4, 3, 0),
    ("mv", 3),
    ("rb", 4, 3, 1),
    ("up", 4),
    ("ra", 0, 1, 0),
    ("ra", 0, 1, 1),
    ("up", 1),
    ("ra", 2, 1, 0),
    ("md", 3),
    ("ra", 2, 2, 1),
    ("ra", 0, 2, 0),
    ("mv", 4),
    ("ra", 0, 2, 1),
    ("mv", 1),
    ("ra", 2, 2, 0),
    ("ga", 3, 0, 1),
    ("ra", 2, 3, 1),
    ("ga", 3, 0, 0),
    ("ra", 0, 3, 0),
    ("ra", 0, 3, 1),
    ("ra", 2, 3, 0),
    ("md", 4),
    ("md", 1),
    ("ga", 3, 1, 0),
    ("ga", 3, 1, 1),
    ("up", 0),
    ("gb", 4, 1, 0),
    ("gb", 4, 1, 1),
    ("up", 2),
    ("bx", 4, 1, 1),
    ("ga", 1, 0, 0),
    ("ga", 1, 0, 1),
    ("mv", 0),
    ("mv", 2),
    ("gb", 4, 2, 1),
    ("ga", 3, 2, 0),
    ("bx", 4, 0, 0),
    ("ga", 1, 1, 1),
    ("ga", 1, 1, 0),
    ("md", 0),
    ("gb", 4, 2, 0),
    ("gb", 4, 3, 1),
    ("ga", 3, 2, 1),
    ("md", 2),
    ("bx", 4, 1, 0),
    ("ga", 1, 2, 1),
    ("ga", 1, 2, 0),
    ("bx", 4, 2, 1),
    ("ga", 3, 3, 0),
    ("ga", 0, 0, 1),
    ("gb", 4, 3, 0),
    ("bx", 4, 0, 1),
    ("bx", 4, 3, 0),
    ("ga", 0, 0, 0),
    ("bx", 4, 3, 1),
    ("ga", 2, 0, 0),
    ("ga", 2, 0, 1),
    ("ga", 0, 1, 1),
    ("ga", 0, 1, 0),
    ("ga", 2, 1, 0),
    ("ga", 2, 1, 1),
    ("ga", 0, 2, 1),
    ("ga", 0, 2, 0),
    ("ga", 1, 3, 0),
    ("bx", 4, 2, 0),
    ("ga", 2, 2, 1),
    ("ga", 2, 2, 0),
    ("ga", 2, 3, 0),
    ("ga", 0, 3, 1),
    ("ga", 0, 3, 0),
    ("ga", 1, 3, 1),
    ("ga", 2, 3, 1),
    ("ga", 3, 3, 1),
    ("end", 4),
)


class Counter:
    def __init__(self):
        self.used = 0

    def take(self):
        self.used += 1
        return self.used - 1


def semaphores_in_all():
    return sum(18 if kind == "a" else 30 for kind, _ in CHUNKS)


def scratch_of(kind, half, rows, slots):
    bf, f32 = jnp.bfloat16, jnp.float32
    block = 2 * rows if kind == "a" else rows
    crossing = 1 if kind == "a" else 4
    return [
        pltpu.VMEM((2, 3, block, half), bf),
        pltpu.VMEM((2, 3, block, half), bf),
        pltpu.VMEM((2, crossing, rows, half), bf),
        pltpu.VMEM((2, crossing, rows, half), bf),
        pltpu.VMEM((2, rows, half), f32),
        pltpu.VMEM((rows, 2 * half), bf),
        pltpu.VMEM((slots, rows // slots, 2 * half), bf),
        pltpu.VMEM((slots, rows // slots, 2 * half), bf),
    ]


PER_CHUNK = 8


def kernel(
    sizes,
    old_ref,
    new_ref,
    count_ref,
    act_hbm,
    grad_hbm,
    master_hbm,
    first_hbm,
    second_hbm,
    master_out,
    first_out,
    second_out,
    weight,
    act_raw,
    act_t,
    grad_raw,
    cot,
    states,
    source,
    load_sem,
    send_sem,
    recv_sem,
    *buffers,
):
    ny, nl, nc, rows, tokens, scale = sizes
    slots = ny * nl * nc
    piece = rows // slots
    block = 2 * rows
    z, xh, y, xl, c = (lax.axis_index(a) for a in AXES)
    me = (y * nl + xl) * nc + c
    dp_row = (z * 2 + xh) * rows

    kinds, halves, starts, parts = [], [], [], []
    at_column = 0
    for k, (kind, half) in enumerate(CHUNKS):
        kinds.append(kind)
        halves.append(half)
        starts.append(at_column)
        parts.append(buffers[k * PER_CHUNK : (k + 1) * PER_CHUNK])
        at_column += 2 * half
    ring_send, ring_recv, cross_send, cross_recv, own, updated, spread, chosen = zip(*parts)

    def columns(k, dr):
        return pl.ds(starts[k] + dr * halves[k], halves[k])

    def both(k):
        return pl.ds(starts[k], 2 * halves[k])

    def device(zz=None, xx=None, slot=None):
        yy, ll, cc = slot if slot is not None else (y, xl, c)
        return (z if zz is None else zz, xh if xx is None else xx, yy, ll, cc)

    z_next = lax.rem(z + 1, 4)
    z_prev = lax.rem(z + 3, 4)
    toward = (device(zz=z_next), device(zz=z_prev))
    across = device(xx=1 - xh)
    others = []
    for jy in range(ny):
        for jl in range(nl):
            for jc in range(nc):
                if jy or jl or jc:
                    slot = (lax.rem(y + jy, ny), lax.rem(xl + jl, nl), lax.rem(c + jc, nc))
                    others.append((device(slot=slot), (slot[0] * nl + slot[1]) * nc + slot[2]))

    loads = []

    def load(src, dst):
        cp = pltpu.make_async_copy(src, dst, load_sem.at[len(loads)])
        cp.start()
        loads.append(cp)
        return cp

    got = {}
    to_load = [tuple(task) for task in PLAN if task[0] in ("mask", "turn")] + [("states",)]

    def load_next():
        if not to_load:
            return
        key = to_load.pop(0)
        got[key] = []
        if key[0] == "mask":
            cols = both(key[1])
            got[key].append(load(grad_hbm.at[:, cols], grad_raw.at[:, cols]))
        elif key[0] == "turn":
            rel = key[1]
            base = lax.rem(z + rel, 4) * block
            for part, at in ((0, xh), (1, 1 - xh)):
                cols = pl.ds(pl.multiple_of(base + at * rows, rows), rows)
                got[key].append(
                    load(act_hbm.at[:, cols], act_raw.at[rel, :, pl.ds(part * rows, rows)])
                )
        else:
            for n, ref in enumerate((master_hbm, first_hbm, second_hbm)):
                got[key].append(load(ref, states.at[n]))

    for _ in range(3):
        load_next()

    def loaded(*key):
        if key in got or key in to_load:
            while key not in got:
                load_next()
            for cp in got.pop(key):
                cp.wait()
            load_next()

    barrier = pltpu.get_barrier_semaphore()
    partners = [toward[0], toward[1], across] + [dev for dev, _ in others]
    for dev in partners:
        pl.semaphore_signal(barrier, inc=1, device_id=dev, device_id_type=MESH)

    live = count_ref[0]

    def find():
        for k in range(slots):
            found = jnp.int32(0)
            for e in range(slots):
                found = jnp.where(new_ref[e] == k, old_ref[e], found)
            source[k] = found

    def enter():
        pl.semaphore_wait(barrier, len(partners))

    def mask(k):
        loaded("mask", k)
        keep = lax.broadcasted_iota(jnp.int32, (tokens, 128), 0) < live
        for j in range(2 * halves[k] // 128):
            cols = pl.ds(starts[k] + j * 128, 128)
            part = grad_raw[:, cols]
            cot[:, cols] = jnp.where(keep, part, jnp.zeros_like(part))

    def turn(rel):
        loaded("turn", rel)

        def one(i, carry):
            at = pl.ds(pl.multiple_of(i * 128, 128), 128)
            act_t[rel, at, :] = act_raw[rel, :, at].T
            return carry

        lax.fori_loop(0, block // 128, one, 0)

    def product(rel, row0, count, cols, write, terms=()):
        step = min(count, 256)

        def one(i, carry):
            at = pl.multiple_of(i * step, step)
            total = jnp.dot(
                act_t[rel, pl.ds(row0 + at, step), :],
                cot[:, cols],
                preferred_element_type=jnp.float32,
            )
            for ref, first in terms:
                total = total + ref[pl.ds(at + first, step), :].astype(jnp.float32)
            write[pl.ds(at, step), :] = total.astype(write.dtype)
            return carry

        lax.fori_loop(0, count // step, one, 0)

    counter, group_counter = Counter(), Counter()
    sends = []
    sent = {}

    def copy_of(src, dst, dev, n, group):
        return pltpu.make_async_remote_copy(
            src_ref=src,
            dst_ref=dst,
            send_sem=send_sem.at[group],
            recv_sem=recv_sem.at[n],
            device_id=dev,
            device_id_type=MESH,
        )

    groups = {}

    def send(src, dst, dev, group, size, whole):
        if group not in groups:
            groups[group] = [group_counter.take(), size]
        n, left = groups[group]
        cp = copy_of(src, dst, dev, counter.take(), n)
        cp.start()
        groups[group][1] = left - 1
        if left == 1:
            sends.append(copy_of(whole, whole, across, 0, n))
        return cp

    def send_group(pairs, pieces):
        n, group = counter.take(), group_counter.take()
        for src, dst, dev in pairs:
            copy_of(src, dst, dev, n, group).start()
        whole = pieces.at[pl.ds(0, slots - 1)]
        cp = copy_of(whole, whole, across, n, group)
        sends.append(cp)
        return cp

    order = ((3, 2, 1, 0), (1, 2, 3, 0))

    def ra(k, s, dr):
        rel, cols = order[dr][s], columns(k, dr)
        if s:
            sent["z", k, dr, s - 1].wait_recv()
            before = ring_recv[k].at[dr, s - 1]
        if s < 3:
            dst = ring_send[k].at[dr, s]
            product(rel, 0, block, cols, dst, ((before, 0),) if s else ())
            sent["z", k, dr, s] = send(
                dst, ring_recv[k].at[dr, s], toward[dr], ("z", k), 6, ring_send[k]
            )
        else:
            far = cross_send[k].at[dr, 0]
            product(rel, rows, rows, cols, far, ((before, rows),))
            sent["x", k, dr] = send(
                far, cross_recv[k].at[dr, 0], across, ("x", k), 2, cross_send[k]
            )
            product(rel, 0, rows, cols, own[k].at[dr], ((before, 0),))

    def xb(k, dr, s):
        far = cross_send[k].at[dr, s]
        product(order[dr][s], rows, rows, columns(k, dr), far)
        sent["x", k, dr, s] = send(
            far, cross_recv[k].at[dr, s], across, ("x", k), 8, cross_send[k]
        )

    def rb(k, s, dr):
        sent["x", k, dr, s].wait_recv()
        terms = [(cross_recv[k].at[dr, s], 0)]
        if s:
            sent["z", k, dr, s - 1].wait_recv()
            terms.append((ring_recv[k].at[dr, s - 1], 0))
        dst = ring_send[k].at[dr, s] if s < 3 else own[k].at[dr]
        product(order[dr][s], 0, rows, columns(k, dr), dst, terms)
        if s < 3:
            sent["z", k, dr, s] = send(
                dst, ring_recv[k].at[dr, s], toward[dr], ("z", k), 6, ring_send[k]
            )

    def up(k):
        loaded("states")
        half = halves[k]
        few = min(rows, 32 * 256 // half)
        for dr in (0, 1):
            if kinds[k] == "a":
                sent["x", k, dr].wait_recv()
            cols = columns(k, dr)

            def one(i, carry, dr=dr, cols=cols):
                at = pl.ds(pl.multiple_of(i * few, few), few)
                total = own[k][dr, at, :]
                if kinds[k] == "a":
                    total = total + cross_recv[k][dr, 0, at, :].astype(jnp.float32)
                new, first, second = adamw(
                    total * scale, states[0, at, cols], states[1, at, cols], states[2, at, cols]
                )
                master_out[at, cols] = new
                first_out[at, cols] = first
                second_out[at, cols] = second
                updated[k][at, pl.ds(dr * half, half)] = new.astype(jnp.bfloat16)
                return carry

            lax.fori_loop(0, rows // few, one, 0)
        sent["spread", k] = send_group(
            [
                (
                    updated[k].at[pl.ds(pl.multiple_of(slot * piece, piece), piece)],
                    spread[k].at[me],
                    dev,
                )
                for dev, slot in others
            ],
            spread[k],
        )
        spread[k][me] = updated[k][pl.ds(pl.multiple_of(me * piece, piece), piece), :]

    def mv(k):
        sent["spread", k].wait_recv()
        for slot in range(slots):
            chosen[k][slot] = spread[k][source[slot]]
        here = (pl.ds(pl.multiple_of(dp_row + me * piece, piece), piece), both(k))
        sent["move", k] = send_group(
            [(chosen[k].at[slot], weight.at[here], dev) for dev, slot in others], chosen[k]
        )
        weight[here] = chosen[k][me]

    def pass_on(at, dev, k, way, size):
        count = size // 2 * (block if kinds[k] == "a" and way == "gz" else rows)
        whole = weight.at[pl.ds(0, count), both(k)]
        return send(weight.at[at], weight.at[at], dev, (way, k), size, whole)

    def md(k):
        sent["move", k].wait_recv()
        here = pl.ds(pl.multiple_of(dp_row, rows), rows)
        for dr in (0, 1):
            at = (here, columns(k, dr))
            if kinds[k] == "a":
                sent["gx", k, dr] = pass_on(at, across, k, "gx", 2)
            else:
                sent["gz", k, dr, 0] = pass_on(at, toward[dr], k, "gz", 6)

    def z_block(s, dr):
        return lax.rem(z + ((4 - s) if dr == 0 else s), 4)

    def ga(k, s, dr):
        row0 = pl.multiple_of(z_block(s, dr) * block, block)
        if s:
            sent["gz", k, dr, s - 1].wait_recv()
        else:
            sent["gx", k, dr].wait_recv()
        if s < 3:
            sent["gz", k, dr, s] = pass_on(
                (pl.ds(row0, block), columns(k, dr)), toward[dr], k, "gz", 6
            )

    def b_rows(k, s, dr):
        row0 = pl.multiple_of((z_block(s, dr) * 2 + xh) * rows, rows)
        return (pl.ds(row0, rows), columns(k, dr))

    def gb(k, s, dr):
        sent["gz", k, dr, s - 1].wait_recv()
        if s < 3:
            sent["gz", k, dr, s] = pass_on(b_rows(k, s, dr), toward[dr], k, "gz", 6)

    def bx(k, s, dr):
        sent["bx", k, dr, s] = pass_on(b_rows(k, s, dr), across, k, "bx", 8)

    def end(k):
        for dr in (0, 1):
            for s in range(4):
                sent["bx", k, dr, s].wait_recv()

    tasks = (find, enter, mask, turn, ra, xb, rb, up, mv, md, ga, gb, bx, end)
    named = {task.__name__: task for task in tasks}
    ended, issued = 0, []
    for name, *given in PLAN:
        with jax.named_scope("_".join([name] + [str(g) for g in given])):
            if name in ("ga", "gb", "md") and len(issued) > 20:
                until = min(issued[-20], ended + 9)
                for cp in sends[ended:until]:
                    cp.wait_send()
                ended = max(ended, until)
            named[name](*given)
        issued.append(len(sends))
    with jax.named_scope("rest"):
        for cp in sends[ended:]:
            cp.wait_send()


def keep(*refs):
    sem = refs[8]
    copies = []
    for src, dst in zip(refs[:4], refs[4:8]):
        half = src.shape[0] // 2
        for row0 in (0, half):
            at = pl.ds(row0, half)
            copies.append(pltpu.make_async_copy(src.at[at], dst.at[at], sem.at[len(copies)]))
    for cp in copies:
        cp.start()
    for cp in copies:
        cp.wait()


def solution(mesh):
    finer = Mesh(mesh.devices.reshape(4, 2, 4, 2, 2), AXES)
    return build(finer)


def build(finer):
    ny, nl, nc = (finer.shape[a] for a in EXPERT)
    slots = ny * nl * nc

    def on_device(act, grad, counts, master, moment1, moment2, old_slot, new_slot):
        tokens, width = act.shape[1], act.shape[2]
        columns = grad.shape[2]
        rows = width // 8
        block = 2 * rows
        bf, f32 = jnp.bfloat16, jnp.float32
        sizes = (ny, nl, nc, rows, tokens, 1.0 / math.sqrt(tokens * 8))
        any_spec = pl.BlockSpec(memory_space=pl.ANY)
        smem = pl.BlockSpec(memory_space=pltpu.SMEM)
        copies = semaphores_in_all()
        state = pltpu.VMEM((rows, columns), f32)
        scratch = [
            pltpu.VMEM((4, tokens, block), bf),
            pltpu.VMEM((4, block, tokens), bf),
            pltpu.VMEM((tokens, columns), bf),
            pltpu.VMEM((tokens, columns), bf),
            pltpu.VMEM((3, rows, columns), f32),
            pltpu.SMEM((slots,), jnp.int32),
            pltpu.SemaphoreType.DMA((len(CHUNKS) + 11,)),
            pltpu.SemaphoreType.DMA((6 * len(CHUNKS),)),
            pltpu.SemaphoreType.DMA((copies,)),
        ]
        for kind, half in CHUNKS:
            scratch += scratch_of(kind, half, rows, slots)
        results = pl.pallas_call(
            functools.partial(kernel, sizes),
            out_shape=(state, state, state, pltpu.VMEM((width, columns), bf)),
            in_specs=[smem, smem, smem] + [any_spec] * 5,
            out_specs=(pl.BlockSpec(memory_space=pltpu.VMEM),) * 4,
            scratch_shapes=scratch,
            compiler_params=pltpu.CompilerParams(
                collective_id=0, has_side_effects=True, vmem_limit_bytes=46 << 20
            ),
            name="step",
        )(
            old_slot,
            new_slot,
            counts[0],
            act[0],
            grad[0],
            master[0],
            moment1[0],
            moment2[0],
        )
        new, first, second, moved = pl.pallas_call(
            keep,
            out_shape=tuple(jax.ShapeDtypeStruct(r.shape, r.dtype) for r in results),
            in_specs=[pl.BlockSpec(memory_space=pltpu.VMEM)] * 4,
            out_specs=(any_spec,) * 4,
            scratch_shapes=[pltpu.SemaphoreType.DMA((8,))],
            compiler_params=pltpu.CompilerParams(vmem_limit_bytes=1 << 20),
            name="keep",
        )(*results)
        return (new[None], first[None], second[None], moved[None])

    in_specs = (
        P(EXPERT, DP, None),
        P(EXPERT, DP, None),
        P(EXPERT, DP),
        P(EXPERT, DP, None),
        P(EXPERT, DP, None),
        P(EXPERT, DP, None),
        P(),
        P(),
    )
    out_specs = (
        P(EXPERT, DP, None),
        P(EXPERT, DP, None),
        P(EXPERT, DP, None),
        P(EXPERT, None, None),
    )
    return jax.shard_map(on_device, mesh=finer, in_specs=in_specs, out_specs=out_specs, check_vma=False)
```
